32 devices in a mesh: size: 4 (over z), gz: 8 (over y, x, core).
Axes of the slice: x: 2, y: 2, z: 4, core: 2. Of those that a mesh axis runs over, the one named last changes fastest.
Arguments:
- tissue: int32 [256, 64, 128], P('gz'), may hold values from 0 to 2
- vessel_pressure: float32 [256, 64, 128], P('gz', 'size'), may hold values from -12 to 12
- cond_table: float32 [3], replicated, may hold values from 0.4 to 1.2
- leak_table: float32 [3], replicated, may hold values from 0.2 to 2
- bind_table: float32 [4, 3], P('size'), may hold values from 0.05 to 1
- hindrance: float32 [4], P('size'), may hold values from 0.2 to 1
- diffusivity: float32 [4], P('size'), may hold values from 0.1 to 0.6
- free_conc: float32 [4, 256, 64, 128], P('size', 'gz'), may hold values from 0 to 2
- bound_conc: float32 [4, 256, 64, 128], P('size', 'gz'), may hold values from 0 to 1
Outputs:
- pressure: float32 [256, 64, 128], P('gz', 'size')
- free_out: float32 [4, 256, 64, 128], P('size', 'gz')
- bound_out: float32 [4, 256, 64, 128], P('size', 'gz')
The draws below stay inside these ranges and needn't reach their ends.
Inputs may be any that keep to these rules, and one draw needn't show every extreme that they name: 0 marks a vessel cell, 1 necrotic tissue, 2 viable tissue.
All inputs are finite; a program needn't handle non-finite values.
Results may differ from the reference program's by a relative error of at most 0.0001.
Values sent between devices are 32-bit elements; how exact they have to be, the bound alone decides.
No kernel may reach another device: no remote copies, remote signals or barrier semaphores. Data moves between devices by JAX's collectives and lax.ppermute only.
A program may use at most 128 MiB of HBM per device.

```python
import math
import jax
import jax.numpy as jnp

NY = 128
ITERS = 2
TSTEPS = 2
NX = 64
NZ = 256
SIZES = 4


def draw_vessel_pressure(key, part):
    depth = (jnp.arange(NZ, dtype=jnp.float32) / NZ)[:, None, None]
    across = (jnp.arange(NX, dtype=jnp.float32) / NX)[None, :, None]
    scale = 1.0 + depth + across
    base = jnp.clip(jax.random.normal(key, (NZ, NX, NY), jnp.float32), -4.0, 4.0)
    return base * scale


def touch_ends(drawn, rng, low, top_value):
    spot = [jax.random.randint(jax.random.fold_in(rng, axis), (), 0, length) for axis, length in enumerate(drawn.shape)]
    widest = drawn.shape.index(max(drawn.shape))
    neighbour = spot[:widest] + [(spot[widest] + 1) % drawn.shape[widest]] + spot[widest + 1:]
    return drawn.at[tuple(spot)].set(low).at[tuple(neighbour)].set(top_value)


def block_levels(key, extent, pieces, smallest, largest):
    factor_of, own = 1.0, jax.random.fold_in(key, 6)
    for dim, blocks in pieces:
        draws = jnp.exp(jax.random.uniform(jax.random.fold_in(own, dim), (blocks,), jnp.float32, smallest / len(pieces), largest / len(pieces)))
        factor_of = factor_of * jnp.repeat(draws, extent[dim] // blocks).reshape([-1 if axis == dim else 1 for axis in range(len(extent))])
    return factor_of


def setup_inputs(seed: int = 0) -> dict:
    arg_keys = jax.random.split(jax.random.key(seed), 10)
    return {
        "tissue": touch_ends(jax.random.randint(arg_keys[0], (NZ, NX, NY), 0, 3), jax.random.fold_in(arg_keys[0], 1), 0, 2).astype(jnp.int32),
        "vessel_pressure": draw_vessel_pressure(jax.random.fold_in(arg_keys[9], 71), 0),
        "cond_table": jnp.clip(jnp.exp(jax.random.uniform(arg_keys[2], (3,), jnp.float32, math.log(0.4), math.log(1.2))), 0.4, 1.2),
        "leak_table": jnp.clip(jnp.exp(jax.random.uniform(arg_keys[3], (3,), jnp.float32, math.log(0.2), math.log(2.0))), 0.2, 2.0),
        "bind_table": jnp.clip(jnp.exp(math.log(1.0) - 2.9957323 * jax.random.uniform(arg_keys[4], (SIZES, 3), jnp.float32) ** block_levels(arg_keys[4], (SIZES, 3), ((0, 4),), -0.2, 0.2)), 0.05, 1.0),
        "hindrance": jnp.clip(jnp.exp(math.log(1.0) - 1.609438 * jax.random.uniform(arg_keys[5], (SIZES,), jnp.float32) ** block_levels(arg_keys[5], (SIZES,), ((0, 4),), -0.2, 0.2)), 0.2, 1.0),
        "diffusivity": jnp.clip(jnp.exp(math.log(0.6) - 1.7917595 * jax.random.uniform(arg_keys[6], (SIZES,), jnp.float32) ** block_levels(arg_keys[6], (SIZES,), ((0, 4),), -0.2, 0.2)), 0.1, 0.6),
        "free_conc": jnp.clip(2.0 * jax.random.uniform(arg_keys[7], (SIZES, NZ, NX, NY), jnp.float32) ** block_levels(arg_keys[7], (SIZES, NZ, NX, NY), ((0, 4), (1, 8)), -0.2, 0.2), 0.0, 2.0),
        "bound_conc": jnp.clip(1.0 * jax.random.uniform(arg_keys[8], (SIZES, NZ, NX, NY), jnp.float32) ** block_levels(arg_keys[8], (SIZES, NZ, NX, NY), ((0, 4), (1, 8)), -0.2, 0.2), 0.0, 1.0),
    }


time_step = 0.1


def lookup(table, labels):
    return jnp.where(labels == 0, table[0], jnp.where(labels == 1, table[1], table[2]))


def neighbours(padded):
    total = padded[2:, 1:-1, 1:-1] + padded[:-2, 1:-1, 1:-1]
    total = total + padded[1:-1, 2:, 1:-1] + padded[1:-1, :-2, 1:-1]
    total = total + padded[1:-1, 1:-1, 2:] + padded[1:-1, 1:-1, :-2]
    return total


def apply_operator(vector, conduct, leak):
    scaled = conduct * vector
    padded = jnp.pad(scaled, 1)
    return conduct * (6.0 * scaled - neighbours(padded)) + leak * vector


def along_line(array, along_dim):
    return array[tuple(slice(None) if k == along_dim else slice(1, -1) for k in range(3))]


def lower_part(array, along_dim):
    return array[tuple(slice(0, -1) if k == along_dim else slice(None) for k in range(3))]


def upper_part(array, along_dim):
    return array[tuple(slice(1, None) if k == along_dim else slice(None) for k in range(3))]


def transport_step(conc_pad, fields_pad, hinder, diffuse):
    divergence = None
    for along_dim in range(3):
        conc_line = along_line(conc_pad, along_dim)
        press_line = along_line(fields_pad[0], along_dim)
        cond_line = along_line(fields_pad[1], along_dim)
        conc_low = lower_part(conc_line, along_dim)
        conc_high = upper_part(conc_line, along_dim)
        velocity = hinder * lower_part(cond_line, along_dim) * upper_part(cond_line, along_dim) * (lower_part(press_line, along_dim) - upper_part(press_line, along_dim))
        flux = jnp.maximum(velocity, 0.0) * conc_low + jnp.minimum(velocity, 0.0) * conc_high + diffuse * (conc_low - conc_high)
        term = upper_part(flux, along_dim) - lower_part(flux, along_dim)
        divergence = term if divergence is None else divergence + term
    conc = conc_pad[1:-1, 1:-1, 1:-1]
    rate = fields_pad[2][1:-1, 1:-1, 1:-1]
    bind = rate * conc
    return conc - time_step * (divergence + bind), bind


def reference(tissue, vessel_pressure, cond_table, leak_table, bind_table, hindrance, diffusivity, free_conc, bound_conc):
    conduct = lookup(cond_table, tissue)
    leak = lookup(leak_table, tissue)
    diag = 6.0 * conduct * conduct + leak
    source = leak * vessel_pressure
    solution = jnp.zeros_like(source)
    residual = source
    precond = residual / diag
    direction = precond
    rho_now = jnp.sum(residual * precond)
    for iteration in range(ITERS):
        image = apply_operator(direction, conduct, leak)
        alpha = rho_now / jnp.sum(direction * image)
        solution = solution + alpha * direction
        residual = residual - alpha * image
        if iteration + 1 < ITERS:
            precond = residual / diag
            rho_next = jnp.sum(residual * precond)
            direction = precond + (rho_next / rho_now) * direction
            rho_now = rho_next
    free_list = []
    bound_list = []
    for class_index in range(SIZES):
        rate = lookup(bind_table[class_index], tissue)
        fields_pad = jnp.pad(jnp.stack([solution, conduct, rate]), ((0, 0), (1, 1), (1, 1), (1, 1)))
        conc = free_conc[class_index]
        bound = bound_conc[class_index]
        for sweep in range(TSTEPS):
            conc, bind = transport_step(jnp.pad(conc, 1), fields_pad, hindrance[class_index], diffusivity[class_index])
            bound = bound + time_step * bind
        free_list.append(conc)
        bound_list.append(bound)
    return solution, jnp.stack(free_list), jnp.stack(bound_list)
```

```python
import functools
import jax
import jax.numpy as jnp
from jax import lax
from jax.experimental import pallas as pl
from jax.experimental.pallas import tpu as pltpu
from jax.sharding import PartitionSpec as P

TSTEPS = 2
HALO = TSTEPS + 1
DT = 0.1


def select(labels, values):
    return jnp.where(labels == 0, values[0], jnp.where(labels == 1, values[1], values[2]))


def following(cells, axis):
    return pltpu.roll(cells, cells.shape[axis] - 1, axis)


def preceding(cells, axis):
    return pltpu.roll(cells, 1, axis)


def edges(shape):
    row = lax.broadcasted_iota(jnp.int32, shape, 0)
    lane = lax.broadcasted_iota(jnp.int32, shape, 1)
    return (row == 0, row == shape[0] - 1), (lane == 0, lane == shape[1] - 1)


def plane_sum(cells, ends):
    total = None
    for axis in range(2):
        low, high = ends[axis]
        part = jnp.where(high, 0.0, following(cells, axis)) + jnp.where(low, 0.0, preceding(cells, axis))
        total = part if total is None else total + part
    return total


def krylov_kernel(parts, rim, cond_t, leak_t, vp, *refs):
    outer = refs[: parts - 1]
    inner = refs[parts - 1 : 2 * parts - 2]
    vp_low, vp_high, tissue, tis_low, tis_high, p_out, u_out, c_out, sums, scaled = refs[2 * parts - 2 :]
    layers, width, _ = vp.shape
    me = lax.axis_index("size")
    slab = lax.axis_index("gz")
    slabs = lax.axis_size("gz")
    cond = [cond_t[i] for i in range(3)]
    leak = [leak_t[i] for i in range(3)]
    diag = [6.0 * c * c + k for c, k in zip(cond, leak)]
    ratio = [k / d for k, d in zip(leak, diag)]
    gain = [c / d for c, d in zip(cond, diag)]
    has_low = (slab > 0).astype(jnp.float32)
    has_high = (slab < slabs - 1).astype(jnp.float32)

    def place(layer, column, pressure, labels, valid):
        spot = pl.ds(column, width)
        c = select(labels, cond)
        if valid is not None:
            c = c * valid
        p = pressure * select(labels, ratio)
        c_out[layer, spot, :] = c
        p_out[layer, spot, :] = p
        scaled[layer, spot, :] = c * p

    for k in range(parts):
        column = pl.multiple_of(lax.rem(me - k + parts, parts) * width, width)
        spot = pl.ds(column, width)

        def fill(first, count, source, offset):
            def body(i, carry):
                place(i + (first + HALO), column, source[i + offset], tissue[i + first, spot, :], None)
                return carry

            lax.fori_loop(0, count, body, 0, unroll=2)

        if k == 0:
            fill(0, layers, vp, 0)
        else:
            fill(0, rim, outer[k - 1], 0)
            fill(rim, layers - 2 * rim, inner[k - 1], 0)
            fill(layers - rim, rim, outer[k - 1], rim)
        for j in range(HALO):
            place(j, column, vp_low[k, j], tis_low[j, spot, :], has_low)
            place(layers + HALO + j, column, vp_high[k, j], tis_high[j, spot, :], has_high)

    shape = tissue.shape[1:]
    ends = edges(shape)

    def image(layer, labels, valid):
        q = scaled[layer]
        around = plane_sum(q, ends) + scaled[layer - 1] + scaled[layer + 1]
        g = select(labels, gain)
        if valid is not None:
            g = g * valid
        u_out[layer] = g * (6.0 * q - around) + select(labels, ratio) * p_out[layer]

    for j in range(1, HALO):
        image(j, tis_low[j], has_low)
        image(layers + HALO + HALO - 1 - j, tis_high[HALO - 1 - j], has_high)

    def middle(i, carry):
        image(i + HALO, tissue[i], None)
        return carry

    lax.fori_loop(0, layers, middle, 0, unroll=2)

    def products(i, carry):
        layer = i + HALO
        labels = tissue[i]
        p, u = p_out[layer], u_out[layer]
        c = c_out[layer]
        d = select(labels, diag)
        du = d * u
        q = c * u
        vertical = c_out[layer - 1] * u_out[layer - 1] + c_out[layer + 1] * u_out[layer + 1]
        energy = select(labels, leak) * u * u + q * (6.0 * q - plane_sum(q, ends) - vertical)
        terms = (d * p * p, du * p, du * u, energy)
        return tuple(a + t.reshape(-1, 8, t.shape[-1]).sum(0) for a, t in zip(carry, terms))

    zero = jnp.zeros((8, shape[1]), jnp.float32)
    totals = lax.fori_loop(0, layers, products, (zero,) * 4)
    sums[...] = jnp.concatenate([t.sum(0, keepdims=True) for t in totals] + [jnp.zeros((4, shape[1]), jnp.float32)], 0)


def transport_kernel(width, bind_t, hinder_t, diffuse_t, sums, p0, u0, cond, tissue, tis_low, tis_high, conc, conc_low, conc_high, bound, pressure, free_out, bound_out, press, first, *coef):
    layers = conc.shape[0]
    shape = conc.shape[1:]
    me = lax.axis_index("size")
    slab = lax.axis_index("gz")
    slabs = lax.axis_size("gz")
    has_low = (slab > 0).astype(jnp.float32)
    has_high = (slab < slabs - 1).astype(jnp.float32)
    rho, drop, second, third = [jnp.sum(sums[i : i + 1, :], axis=1, keepdims=True) for i in range(4)]
    alpha = rho / drop
    rho_next = alpha * alpha * second - rho
    beta = rho_next / rho
    curve = drop - 2.0 * alpha * second + alpha * alpha * third - beta * rho_next / alpha
    alpha_next = rho_next / curve
    on_p = alpha + alpha_next * (1.0 + beta)
    on_u = -alpha_next * alpha
    on_p = jnp.broadcast_to(on_p, (8, shape[1]))[None]
    on_u = jnp.broadcast_to(on_u, (8, shape[1]))[None]
    rate_t = [bind_t[0, i] * DT for i in range(3)]
    hinder = hinder_t[0] * DT
    diffuse = diffuse_t[0] * DT

    def combine(i, carry):
        layer = i + 1
        p = p0[layer].reshape(-1, 8, shape[1])
        u = u0[layer].reshape(-1, 8, shape[1])
        press[layer] = (on_p * p + on_u * u).reshape(shape)
        return carry

    lax.fori_loop(0, layers + 2 * TSTEPS, combine, 0, unroll=2)
    spot = pl.ds(pl.multiple_of(me * width, width), width)

    def own(i, carry):
        pressure[i] = press[i + HALO, spot, :]
        return carry

    lax.fori_loop(0, layers, own, 0, unroll=2)
    ends = edges(shape)

    def face(c, c_next, p, p_next):
        return hinder * c * c_next * (p - p_next)

    def halves(flow):
        out = jnp.maximum(flow, 0.0) + diffuse
        return out, out - flow

    def advance(layer, labels, c_below, c_here, c_above, low_flow, valid):
        k, p = cond[layer], press[layer]
        high_flow = face(k, cond[layer + 1], p, press[layer + 1])
        p_low, n_low = halves(low_flow)
        p_high, n_high = halves(high_flow)
        rate = select(labels, rate_t)
        leave = p_high + n_low + rate
        weights = [p_low, n_high]
        moved = p_low * c_below + n_high * c_above
        for axis in range(2):
            at_low, at_high = ends[axis]
            flow = jnp.where(at_high, 0.0, face(k, following(k, axis), p, following(p, axis)))
            p_high, n_high = halves(flow)
            p_low, n_low = halves(preceding(flow, axis))
            leave = leave + (p_high + n_low)
            n_high = jnp.where(at_high, 0.0, n_high)
            p_low = jnp.where(at_low, 0.0, p_low)
            weights += [p_low, n_high]
            moved = moved + p_low * preceding(c_here, axis) + n_high * following(c_here, axis)
        stay = 1.0 - leave
        result = stay * c_here + moved
        if valid is not None:
            result = result * valid
        first[layer - TSTEPS] = result
        return high_flow, [stay] + weights

    zero = jnp.zeros(shape, jnp.float32)
    low = face(cond[1], cond[2], press[1], press[2])
    low, _ = advance(TSTEPS, tis_low[HALO - 1], conc_low[0], conc_low[1], conc[0], low, has_low)

    def keep(i, weights):
        for ref, weight in zip(coef, weights):
            ref[i] = weight

    low, weights = advance(HALO, tissue[0], conc_low[1], conc[0], conc[1], low, None)
    keep(0, weights)

    def body(i, low):
        low, weights = advance(i + HALO, tissue[i], conc[i - 1], conc[i], conc[i + 1], low, None)
        keep(i, weights)
        return low

    low = lax.fori_loop(1, layers - 1, body, low)
    low, weights = advance(layers - 1 + HALO, tissue[layers - 1], conc[layers - 2], conc[layers - 1], conc_high[0], low, None)
    keep(layers - 1, weights)
    advance(layers + HALO, tis_high[0], conc[layers - 1], conc_high[0], conc_high[1], low, has_high)

    def last(i, carry):
        here = first[i + 1]
        stay, z_low, z_high, x_low, x_high, y_low, y_high = [ref[i] for ref in coef]
        result = stay * here + z_low * first[i] + z_high * first[i + 2]
        result = result + x_low * preceding(here, 0) + x_high * following(here, 0)
        free_out[i] = result + y_low * preceding(here, 1) + y_high * following(here, 1)
        bound_out[i] = bound[i] + select(tissue[i], rate_t) * (conc[i] + here)
        return carry

    lax.fori_loop(0, layers, last, 0)


def shifts(array, axis):
    count = lax.axis_size(axis)
    return [lax.ppermute(array, axis, [(i, (i + k) % count) for i in range(count)]) for k in range(1, count)]


def across(low, high):
    count = lax.axis_size("gz")
    from_low = lax.ppermute(high, "gz", [(i, i + 1) for i in range(count - 1)])
    from_high = lax.ppermute(low, "gz", [(i + 1, i) for i in range(count - 1)])
    return from_low, from_high


def total_over(array, axis):
    count = lax.axis_size(axis)
    step = 1
    while step < count:
        array = array + lax.ppermute(array, axis, [(i, i ^ step) for i in range(count)])
        step *= 2
    return array


def smem():
    return pl.BlockSpec(memory_space=pltpu.SMEM)


def vmem():
    return pl.BlockSpec(memory_space=pltpu.VMEM)


def local(tissue, vessel_pressure, cond_table, leak_table, bind_table, hindrance, diffusivity, free_conc, bound_conc):
    layers, width, lanes = vessel_pressure.shape
    rows = tissue.shape[1]
    parts = rows // width
    rim = max(HALO, layers // 4)
    conc, bound = free_conc[0], bound_conc[0]
    rims = jnp.concatenate([vessel_pressure[:rim], vessel_pressure[layers - rim :]], 0)
    outer = shifts(rims, "size")
    inner = shifts(vessel_pressure[rim : layers - rim], "size")
    tis_low, tis_high = across(tissue[:HALO], tissue[layers - HALO :])
    conc_low, conc_high = across(conc[:TSTEPS], conc[layers - TSTEPS :])
    blocks = [rims] + outer
    vp_low, vp_high = across(jnp.stack([b[:HALO] for b in blocks]), jnp.stack([b[2 * rim - HALO :] for b in blocks]))
    extended = jax.ShapeDtypeStruct((layers + 2 * HALO, rows, lanes), jnp.float32)
    p0, u0, cond, sums = pl.pallas_call(
        functools.partial(krylov_kernel, parts, rim),
        out_shape=(extended, extended, extended, jax.ShapeDtypeStruct((8, lanes), jnp.float32)),
        in_specs=[smem()] * 2 + [vmem()] * (2 * parts + 4),
        out_specs=(vmem(),) * 4,
        scratch_shapes=[pltpu.VMEM(extended.shape, jnp.float32)],
        name="krylov",
    )(cond_table, leak_table, vessel_pressure, *outer, *inner, vp_low, vp_high, tissue, tis_low, tis_high)
    sums = total_over(sums, "gz")
    slab = jax.ShapeDtypeStruct((layers, rows, lanes), jnp.float32)
    pressure, free, bound = pl.pallas_call(
        functools.partial(transport_kernel, width),
        out_shape=(jax.ShapeDtypeStruct(vessel_pressure.shape, jnp.float32), slab, slab),
        in_specs=[smem()] * 3 + [vmem()] * 11,
        out_specs=(vmem(),) * 3,
        scratch_shapes=[pltpu.VMEM(extended.shape, jnp.float32), pltpu.VMEM((layers + 2, rows, lanes), jnp.float32)]
        + [pltpu.VMEM(slab.shape, jnp.float32)] * 7,
        name="transport",
    )(bind_table, hindrance, diffusivity, sums, p0, u0, cond, tissue, tis_low, tis_high, conc, conc_low, conc_high, bound)
    return pressure, free[None], bound[None]


def solution(mesh):
    return jax.shard_map(
        local,
        mesh=mesh,
        in_specs=(
            P("gz", None, None),
            P("gz", "size", None),
            P(),
            P(),
            P("size", None),
            P("size"),
            P("size"),
            P("size", "gz", None, None),
            P("size", "gz", None, None),
        ),
        out_specs=(P("gz", "size", None), P("size", "gz", None, None), P("size", "gz", None, None)),
        check_vma=False,
    )
```

```python
import functools
import math
import jax
import jax.numpy as jnp
from jax import lax
from jax.experimental import pallas as pl
from jax.experimental.pallas import tpu as pltpu
from jax.sharding import PartitionSpec as P

TSTEPS = 2
HALO = TSTEPS + 1
DT = 0.1


def select(labels, values):
    return jnp.where(labels == 0, values[0], jnp.where(labels == 1, values[1], values[2]))


def following(cells, axis):
    return pltpu.roll(cells, cells.shape[axis] - 1, axis)


def preceding(cells, axis):
    return pltpu.roll(cells, 1, axis)


def edges(shape):
    row = lax.broadcasted_iota(jnp.int32, shape, 0)
    lane = lax.broadcasted_iota(jnp.int32, shape, 1)
    return (row == 0, row == shape[0] - 1), (lane == 0, lane == shape[1] - 1)


def inside():
    slab = lax.axis_index("gz")
    has_low = (slab > 0).astype(jnp.float32)
    has_high = (slab < lax.axis_size("gz") - 1).astype(jnp.float32)
    return has_low, has_high


def tables(cond_t, leak_t):
    cond = [cond_t[i] for i in range(3)]
    leak = [leak_t[i] for i in range(3)]
    diag = [6.0 * c * c + k for c, k in zip(cond, leak)]
    ratio = [k / d for k, d in zip(leak, diag)]
    gain = [c / d for c, d in zip(cond, diag)]
    return cond, leak, diag, ratio, gain


def image(layer, labels, valid, ends, gain, ratio, p0, scaled, u0):
    q = scaled[layer]
    around = scaled[layer - 1] + scaled[layer + 1]
    for axis in range(2):
        low, high = ends[axis]
        around = around + jnp.where(high, 0.0, following(q, axis))
        around = around + jnp.where(low, 0.0, preceding(q, axis))
    g = select(labels, gain)
    if valid is not None:
        g = g * valid
    u0[layer] = g * (6.0 * q - around) + select(labels, ratio) * p0[layer]


def products(first, count, totals, ends, tissue, leak, diag, p0, u0, cond):
    def body(i, carry):
        layer = i + HALO
        labels = tissue[i]
        p, u = p0[layer], u0[layer]
        d = select(labels, diag)
        du = d * u
        q = cond[layer] * u
        ahead = jnp.where(ends[0][1], 0.0, following(q, 0)) + jnp.where(ends[1][1], 0.0, following(q, 1))
        vertical = cond[layer - 1] * u0[layer - 1] + cond[layer + 1] * u0[layer + 1]
        energy = select(labels, leak) * u * u + q * (6.0 * q - 2.0 * ahead - vertical)
        terms = (d * p * p, du * p, du * u, energy)
        return tuple(a + t.reshape(-1, 8, t.shape[-1]).sum(0) for a, t in zip(carry, terms))

    return lax.fori_loop(first, first + count, body, totals)


def rim_kernel(parts, rim, cond_t, leak_t, bind_t, hinder_t, vp, *refs):
    outer = refs[: parts - 1]
    from_low, from_high, tissue, conc, p0, scaled, u0, cond, sums, kx, ky, kz, rate, wide = refs[parts - 1 :]
    layers, width, _ = vp.shape
    rows = tissue.shape[1]
    me = lax.axis_index("size")
    has_low, has_high = inside()
    cond_v, leak_v, diag_v, ratio_v, gain_v = tables(cond_t, leak_t)
    rate_v = [bind_t[0, i] * DT for i in range(3)]
    hinder = hinder_t[0] * DT
    tis_at = parts * HALO * width
    conc_at = tis_at + HALO * rows

    def place(layer, spot, pressure, labels):
        p = pressure * select(labels, ratio_v)
        p0[layer, spot, :] = p
        scaled[layer, spot, :] = select(labels, cond_v) * p

    for k in range(parts):
        spot = pl.ds(pl.multiple_of(lax.rem(me - k + parts, parts) * width, width), width)
        source = vp if k == 0 else outer[k - 1]
        top = layers - rim if k == 0 else rim

        def fill(i, carry):
            place(i + HALO, spot, source[i], tissue[i, spot, :])
            place(i + (layers - rim + HALO), spot, source[i + top], tissue[i + (layers - rim), spot, :])
            return carry

        lax.fori_loop(0, rim, fill, 0, unroll=2)
        for j in range(HALO):
            at = (k * HALO + j) * width
            for side, layer in ((from_low, j), (from_high, layers + HALO + j)):
                labels = side[pl.ds(pl.multiple_of(tis_at + j * rows + spot.start, width), width), :]
                place(layer, spot, side[at : at + width, :], labels)

    def halo_labels(side, j):
        return side[tis_at + j * rows : tis_at + (j + 1) * rows, :]

    for j in range(HALO):
        cond[j] = select(halo_labels(from_low, j), cond_v) * has_low
        cond[layers + HALO + j] = select(halo_labels(from_high, j), cond_v) * has_high
    for j in range(TSTEPS):
        wide[j] = from_low[conc_at + j * rows : conc_at + (j + 1) * rows, :]
        wide[layers + TSTEPS + j] = from_high[conc_at + j * rows : conc_at + (j + 1) * rows, :]
    rate[0] = select(halo_labels(from_low, HALO - 1), rate_v)
    rate[layers + 1] = select(halo_labels(from_high, 0), rate_v)

    def own(i, carry):
        labels = tissue[i]
        cond[i + HALO] = select(labels, cond_v)
        rate[i + 1] = select(labels, rate_v)
        wide[i + TSTEPS] = conc[i]
        return carry

    lax.fori_loop(0, layers, own, 0, unroll=2)
    ends = edges(tissue.shape[1:])

    def faces(i, carry):
        c = cond[i + 1]
        scaled_c = hinder * c
        kz[i] = scaled_c * cond[i + 2]
        kx[i] = jnp.where(ends[0][1], 0.0, scaled_c * following(c, 0))
        ky[i] = jnp.where(ends[1][1], 0.0, scaled_c * following(c, 1))
        return carry

    lax.fori_loop(0, layers + TSTEPS + 1, faces, 0)

    for j in range(1, HALO):
        image(j, halo_labels(from_low, j), has_low, ends, gain_v, ratio_v, p0, scaled, u0)
        back = HALO - 1 - j
        image(layers + HALO + back, halo_labels(from_high, back), has_high, ends, gain_v, ratio_v, p0, scaled, u0)

    def both(i, carry):
        image(i + HALO, tissue[i], None, ends, gain_v, ratio_v, p0, scaled, u0)
        j = layers - 1 - i
        image(j + HALO, tissue[j], None, ends, gain_v, ratio_v, p0, scaled, u0)
        return carry

    lax.fori_loop(0, rim - 1, both, 0)
    zero = jnp.zeros((8, tissue.shape[2]), jnp.float32)
    fixed = (ends, tissue, leak_v, diag_v, p0, u0, cond)
    totals = products(0, rim - 2, (zero,) * 4, *fixed)
    totals = products(layers - rim + 2, rim - 2, totals, *fixed)
    for i in range(4):
        sums[i] = totals[i]


def core_kernel(parts, rim, cond_t, leak_t, vp, *refs):
    inner = refs[: parts - 1]
    tissue, cond, part, _, _, _, p0, scaled, u0, sums = refs[parts - 1 :]
    layers, width, _ = vp.shape
    me = lax.axis_index("size")
    cond_v, leak_v, diag_v, ratio_v, gain_v = tables(cond_t, leak_t)
    for k in range(parts):
        spot = pl.ds(pl.multiple_of(lax.rem(me - k + parts, parts) * width, width), width)
        source = vp if k == 0 else inner[k - 1]
        start = rim if k == 0 else 0

        def fill(i, carry):
            labels = tissue[i + rim, spot, :]
            p = source[i + start] * select(labels, ratio_v)
            p0[i + (rim + HALO), spot, :] = p
            scaled[i + (rim + HALO), spot, :] = select(labels, cond_v) * p
            return carry

        lax.fori_loop(0, layers - 2 * rim, fill, 0, unroll=2)
    ends = edges(tissue.shape[1:])

    def middle(i, carry):
        image(i + HALO, tissue[i], None, ends, gain_v, ratio_v, p0, scaled, u0)
        return carry

    lax.fori_loop(rim - 1, layers - rim + 1, middle, 0, unroll=2)
    totals = tuple(part[i] for i in range(4))
    totals = products(rim - 2, layers - 2 * rim + 4, totals, ends, tissue, leak_v, diag_v, p0, u0, cond)
    sums[...] = jnp.concatenate([t.sum(0, keepdims=True) for t in totals] * 2, 0)


def transport_kernel(width, diffuse_t, mine, theirs, p0, u0, kx, ky, kz, rate, wide, bound, pressure, free_out, bound_out, first, *coef):
    layers, rows, lanes = bound.shape
    me = lax.axis_index("size")
    has_low, has_high = inside()
    sums = mine[...] + theirs[...]
    rho, drop, second, third = [jnp.sum(sums[i : i + 1, :], axis=1, keepdims=True) for i in range(4)]
    alpha = rho / drop
    rho_next = alpha * alpha * second - rho
    beta = rho_next / rho
    curve = drop - 2.0 * alpha * second + alpha * alpha * third - beta * rho_next / alpha
    alpha_next = rho_next / curve
    on_p = jnp.broadcast_to(alpha + alpha_next * (1.0 + beta), (8, lanes))[None]
    on_u = jnp.broadcast_to(-alpha_next * alpha, (8, lanes))[None]
    diffuse = diffuse_t[0] * DT

    def combine(p, u):
        shape = p.shape
        return (on_p * p.reshape(-1, 8, lanes) + on_u * u.reshape(-1, 8, lanes)).reshape(shape)

    spot = pl.ds(pl.multiple_of(me * width, width), width)

    def own(i, carry):
        pressure[i] = combine(p0[i + HALO, spot, :], u0[i + HALO, spot, :])
        return carry

    lax.fori_loop(0, layers, own, 0, unroll=4)
    ends = edges((rows, lanes))

    def halves(flow):
        out = jnp.maximum(flow, 0.0) + diffuse
        return out, out - flow

    def advance(i, carry):
        here, low_flow = carry
        above = combine(p0[i + HALO], u0[i + HALO])
        conc = wide[i + 1]
        high_flow = kz[i + 1] * (here - above)
        p_low, n_low = halves(low_flow)
        p_high, n_high = halves(high_flow)
        leave = p_high + n_low + rate[i]
        weights = [p_low, n_high]
        moved = p_low * wide[i] + n_high * wide[i + 2]
        for axis, face in ((0, kx), (1, ky)):
            at_low, at_high = ends[axis]
            flow = face[i + 1] * (here - following(here, axis))
            p_high, n_high = halves(flow)
            p_low, n_low = halves(preceding(flow, axis))
            leave = leave + (p_high + n_low)
            n_high = jnp.where(at_high, 0.0, n_high)
            p_low = jnp.where(at_low, 0.0, p_low)
            weights += [p_low, n_high]
            moved = moved + p_low * preceding(conc, axis) + n_high * following(conc, axis)
        stay = 1.0 - leave
        valid = jnp.where(i == 0, has_low, jnp.where(i == layers + 1, has_high, 1.0))
        first[i] = (stay * conc + moved) * valid
        slot = lax.rem(i, 2)
        for ref, weight in zip(coef, [stay] + weights):
            ref[slot] = weight
        return above, high_flow

    start = combine(p0[TSTEPS], u0[TSTEPS])
    carry = (start, kz[0] * (combine(p0[1], u0[1]) - start))
    carry = lax.fori_loop(0, 2, advance, carry)

    def body(i, carry):
        here = first[i - 1]
        slot = lax.rem(i - 1, 2)
        old = [ref[slot] for ref in coef]
        carry = advance(i, carry)
        stay, z_low, z_high, x_low, x_high, y_low, y_high = old
        result = stay * here + z_low * first[i - 2] + z_high * first[i]
        result = result + x_low * preceding(here, 0) + x_high * following(here, 0)
        free_out[i - 2] = result + y_low * preceding(here, 1) + y_high * following(here, 1)
        bound_out[i - 2] = bound[i - 2] + rate[i - 1] * (wide[i] + here)
        return carry

    lax.fori_loop(2, layers + 2, body, carry)


def shifts(array, axis):
    count = lax.axis_size(axis)
    return [lax.ppermute(array, axis, [(i, (i + k) % count) for i in range(count)]) for k in range(1, count)]


def across(low, high):
    count = lax.axis_size("gz")
    from_low = lax.ppermute(high, "gz", [(i, i + 1) for i in range(count - 1)])
    from_high = lax.ppermute(low, "gz", [(i + 1, i) for i in range(count - 1)])
    return from_low, from_high


def total_over(array, axis):
    count = lax.axis_size(axis)
    step = 1
    while True:
        other = lax.ppermute(array, axis, [(i, i ^ step) for i in range(count)])
        step *= 2
        if step == count:
            return array, other
        array = array + other


def smem():
    return pl.BlockSpec(memory_space=pltpu.SMEM)


def vmem():
    return pl.BlockSpec(memory_space=pltpu.VMEM)


def f32(*shape):
    return jax.ShapeDtypeStruct(shape, jnp.float32)


def call(kernel, name, outs, scalars, arrays, scratch=(), aliases={}):
    size = sum(4 * math.prod(a.shape) for a in list(outs) + list(arrays) + list(scratch))
    return pl.pallas_call(
        kernel,
        out_shape=tuple(outs),
        in_specs=[smem()] * len(scalars) + [vmem()] * len(arrays),
        out_specs=(vmem(),) * len(outs),
        scratch_shapes=[pltpu.VMEM(s.shape, s.dtype) for s in scratch],
        input_output_aliases=aliases,
        compiler_params=pltpu.CompilerParams(vmem_limit_bytes=size + (4 << 20)),
        name=name,
    )(*scalars, *arrays)


def local(tissue, vessel_pressure, cond_table, leak_table, bind_table, hindrance, diffusivity, free_conc, bound_conc):
    layers, width, lanes = vessel_pressure.shape
    rows = tissue.shape[1]
    parts = rows // width
    rim = max(HALO, layers // 4)
    conc, bound = free_conc[0], bound_conc[0]
    rims = jnp.concatenate([vessel_pressure[:rim], vessel_pressure[layers - rim :]], 0)
    outer = shifts(rims, "size")
    inner = shifts(vessel_pressure[rim : layers - rim], "size")
    blocks = [rims] + outer

    def payload(pieces, labels, cells):
        arrays = pieces + [labels.astype(jnp.float32), cells]
        return jnp.concatenate([a.reshape(-1, lanes) for a in arrays], 0)

    low = payload([b[:HALO] for b in blocks], tissue[:HALO], conc[:TSTEPS])
    high = payload([b[2 * rim - HALO :] for b in blocks], tissue[layers - HALO :], conc[layers - TSTEPS :])
    from_low, from_high = across(low, high)
    extended = f32(layers + 2 * HALO, rows, lanes)
    stepped = f32(layers + 2, rows, lanes)
    faces = f32(layers + TSTEPS + 1, rows, lanes)
    p0, scaled, u0, cond, part, kx, ky, kz, rate, wide = call(
        functools.partial(rim_kernel, parts, rim),
        "rim",
        [extended] * 4 + [f32(4, 8, lanes), faces, faces, faces, stepped, f32(layers + 2 * TSTEPS, rows, lanes)],
        [cond_table, leak_table, bind_table, hindrance],
        [vessel_pressure, *outer, from_low, from_high, tissue, conc],
    )
    p0, scaled, u0, sums = call(
        functools.partial(core_kernel, parts, rim),
        "core",
        [extended] * 3 + [f32(8, lanes)],
        [cond_table, leak_table],
        [vessel_pressure, *inner, tissue, cond, part, p0, scaled, u0],
        aliases={2 + parts + 3 + i: i for i in range(3)},
    )
    mine, theirs = total_over(sums, "gz")
    slab = f32(layers, rows, lanes)
    pressure, free, bound = call(
        functools.partial(transport_kernel, width),
        "transport",
        [f32(layers, width, lanes), slab, slab],
        [diffusivity],
        [mine, theirs, p0, u0, kx, ky, kz, rate, wide, bound],
        scratch=[stepped] + [f32(2, rows, lanes)] * 7,
    )
    return pressure, free[None], bound[None]


def solution(mesh):
    return jax.shard_map(
        local,
        mesh=mesh,
        in_specs=(
            P("gz", None, None),
            P("gz", "size", None),
            P(),
            P(),
            P("size", None),
            P("size"),
            P("size"),
            P("size", "gz", None, None),
            P("size", "gz", None, None),
        ),
        out_specs=(P("gz", "size", None), P("size", "gz", None, None), P("size", "gz", None, None)),
        check_vma=False,
    )
```

```python
import functools
import math
import jax
import jax.numpy as jnp
from jax import lax
from jax.experimental import pallas as pl
from jax.experimental.pallas import tpu as pltpu
from jax.sharding import PartitionSpec as P

TSTEPS = 2
HALO = TSTEPS + 1
DT = 0.1


def select(labels, values):
    return jnp.where(labels == 0, values[0], jnp.where(labels == 1, values[1], values[2]))


def following(cells, axis):
    return pltpu.roll(cells, cells.shape[axis] - 1, axis)


def preceding(cells, axis):
    return pltpu.roll(cells, 1, axis)


def edges(shape):
    row = lax.broadcasted_iota(jnp.int32, shape, 0)
    lane = lax.broadcasted_iota(jnp.int32, shape, 1)
    return (row == 0, row == shape[0] - 1), (lane == 0, lane == shape[1] - 1)


def inside():
    slab = lax.axis_index("gz")
    has_low = (slab > 0).astype(jnp.float32)
    has_high = (slab < lax.axis_size("gz") - 1).astype(jnp.float32)
    return has_low, has_high


def tables(cond_t, leak_t):
    cond = [cond_t[i] for i in range(3)]
    leak = [leak_t[i] for i in range(3)]
    diag = [6.0 * c * c + k for c, k in zip(cond, leak)]
    ratio = [k / d for k, d in zip(leak, diag)]
    gain = [c / d for c, d in zip(cond, diag)]
    return cond, leak, diag, ratio, gain


def image(layer, labels, valid, ends, gain, ratio, p0, scaled, u0):
    q = scaled[layer]
    around = scaled[layer - 1] + scaled[layer + 1]
    for axis in range(2):
        low, high = ends[axis]
        around = around + jnp.where(high, 0.0, following(q, axis))
        around = around + jnp.where(low, 0.0, preceding(q, axis))
    g = select(labels, gain)
    if valid is not None:
        g = g * valid
    u0[layer] = g * (6.0 * q - around) + select(labels, ratio) * p0[layer]


def products(first, count, totals, ends, tissue, leak, diag, p0, u0, cond):
    def body(i, carry):
        layer = i + HALO
        labels = tissue[i]
        p, u = p0[layer], u0[layer]
        d = select(labels, diag)
        du = d * u
        q = cond[layer] * u
        ahead = jnp.where(ends[0][1], 0.0, following(q, 0)) + jnp.where(ends[1][1], 0.0, following(q, 1))
        vertical = cond[layer - 1] * u0[layer - 1] + cond[layer + 1] * u0[layer + 1]
        energy = select(labels, leak) * u * u + q * (6.0 * q - 2.0 * ahead - vertical)
        terms = (d * p * p, du * p, du * u, energy)
        return tuple(a + t.reshape(-1, 8, t.shape[-1]).sum(0) for a, t in zip(carry, terms))

    return lax.fori_loop(first, first + count, body, totals)


def rim_kernel(parts, rim, cond_t, leak_t, bind_t, hinder_t, vp, *refs):
    outer = refs[: parts - 1]
    from_low, from_high, tissue, conc, p0, scaled, u0, cond, sums, kx, ky, kz, rate, wide = refs[parts - 1 :]
    layers, width, _ = vp.shape
    rows = tissue.shape[1]
    me = lax.axis_index("size")
    has_low, has_high = inside()
    cond_v, leak_v, diag_v, ratio_v, gain_v = tables(cond_t, leak_t)
    rate_v = [bind_t[0, i] * DT for i in range(3)]
    hinder = hinder_t[0] * DT
    tis_at = parts * HALO * width
    conc_at = tis_at + HALO * rows

    def place(layer, spot, pressure, labels):
        p = pressure * select(labels, ratio_v)
        p0[layer, spot, :] = p
        scaled[layer, spot, :] = select(labels, cond_v) * p

    for k in range(parts):
        spot = pl.ds(pl.multiple_of(lax.rem(me - k + parts, parts) * width, width), width)
        source = vp if k == 0 else outer[k - 1]
        top = layers - rim if k == 0 else rim

        def fill(i, carry):
            place(i + HALO, spot, source[i], tissue[i, spot, :])
            place(i + (layers - rim + HALO), spot, source[i + top], tissue[i + (layers - rim), spot, :])
            return carry

        lax.fori_loop(0, rim, fill, 0, unroll=2)
        for j in range(HALO):
            at = (k * HALO + j) * width
            for side, layer in ((from_low, j), (from_high, layers + HALO + j)):
                labels = side[pl.ds(pl.multiple_of(tis_at + j * rows + spot.start, width), width), :]
                place(layer, spot, side[at : at + width, :], labels)

    def halo_labels(side, j):
        return side[tis_at + j * rows : tis_at + (j + 1) * rows, :]

    for j in range(HALO):
        cond[j] = select(halo_labels(from_low, j), cond_v) * has_low
        cond[layers + HALO + j] = select(halo_labels(from_high, j), cond_v) * has_high
    for j in range(TSTEPS):
        wide[j] = from_low[conc_at + j * rows : conc_at + (j + 1) * rows, :]
        wide[layers + TSTEPS + j] = from_high[conc_at + j * rows : conc_at + (j + 1) * rows, :]
    rate[0] = select(halo_labels(from_low, HALO - 1), rate_v)
    rate[layers + 1] = select(halo_labels(from_high, 0), rate_v)

    def own(i, carry):
        labels = tissue[i]
        cond[i + HALO] = select(labels, cond_v)
        rate[i + 1] = select(labels, rate_v)
        wide[i + TSTEPS] = conc[i]
        return carry

    lax.fori_loop(0, layers, own, 0, unroll=2)
    ends = edges(tissue.shape[1:])

    def faces(i, carry):
        c = cond[i + 1]
        scaled_c = hinder * c
        kz[i] = scaled_c * cond[i + 2]
        kx[i] = jnp.where(ends[0][1], 0.0, scaled_c * following(c, 0))
        ky[i] = jnp.where(ends[1][1], 0.0, scaled_c * following(c, 1))
        return carry

    lax.fori_loop(0, layers + TSTEPS + 1, faces, 0)

    for j in range(1, HALO):
        image(j, halo_labels(from_low, j), has_low, ends, gain_v, ratio_v, p0, scaled, u0)
        back = HALO - 1 - j
        image(layers + HALO + back, halo_labels(from_high, back), has_high, ends, gain_v, ratio_v, p0, scaled, u0)

    def both(i, carry):
        image(i + HALO, tissue[i], None, ends, gain_v, ratio_v, p0, scaled, u0)
        j = layers - 1 - i
        image(j + HALO, tissue[j], None, ends, gain_v, ratio_v, p0, scaled, u0)
        return carry

    lax.fori_loop(0, rim - 1, both, 0)
    zero = jnp.zeros((8, tissue.shape[2]), jnp.float32)
    fixed = (ends, tissue, leak_v, diag_v, p0, u0, cond)
    totals = products(0, rim - 2, (zero,) * 4, *fixed)
    totals = products(layers - rim + 2, rim - 2, totals, *fixed)
    for i in range(4):
        sums[i] = totals[i]


def core_kernel(parts, rim, cond_t, leak_t, vp, *refs):
    inner = refs[: parts - 1]
    tissue, cond, part, _, _, _, p0, scaled, u0, sums = refs[parts - 1 :]
    layers, width, _ = vp.shape
    me = lax.axis_index("size")
    cond_v, leak_v, diag_v, ratio_v, gain_v = tables(cond_t, leak_t)
    for k in range(parts):
        spot = pl.ds(pl.multiple_of(lax.rem(me - k + parts, parts) * width, width), width)
        source = vp if k == 0 else inner[k - 1]
        start = rim if k == 0 else 0

        def fill(i, carry):
            labels = tissue[i + rim, spot, :]
            p = source[i + start] * select(labels, ratio_v)
            p0[i + (rim + HALO), spot, :] = p
            scaled[i + (rim + HALO), spot, :] = select(labels, cond_v) * p
            return carry

        lax.fori_loop(0, layers - 2 * rim, fill, 0, unroll=2)
    ends = edges(tissue.shape[1:])

    def middle(i, carry):
        image(i + HALO, tissue[i], None, ends, gain_v, ratio_v, p0, scaled, u0)
        return carry

    lax.fori_loop(rim - 1, layers - rim + 1, middle, 0, unroll=2)
    totals = tuple(part[i] for i in range(4))
    totals = products(rim - 2, layers - 2 * rim + 4, totals, ends, tissue, leak_v, diag_v, p0, u0, cond)
    sums[...] = jnp.concatenate([t.sum(0, keepdims=True) for t in totals] * 2, 0)


def transport_kernel(width, diffuse_t, mine, theirs, p0, u0, kx, ky, kz, rate, wide, bound, pressure, free_out, bound_out, first, *coef):
    layers, rows, lanes = bound.shape
    me = lax.axis_index("size")
    has_low, has_high = inside()
    sums = mine[...] + theirs[...]
    rho, drop, second, third = [jnp.sum(sums[i : i + 1, :], axis=1, keepdims=True) for i in range(4)]
    alpha = rho / drop
    rho_next = alpha * alpha * second - rho
    beta = rho_next / rho
    curve = drop - 2.0 * alpha * second + alpha * alpha * third - beta * rho_next / alpha
    alpha_next = rho_next / curve
    on_p = jnp.broadcast_to(alpha + alpha_next * (1.0 + beta), (8, lanes))[None]
    on_u = jnp.broadcast_to(-alpha_next * alpha, (8, lanes))[None]
    diffuse = diffuse_t[0] * DT

    def combine(p, u):
        shape = p.shape
        return (on_p * p.reshape(-1, 8, lanes) + on_u * u.reshape(-1, 8, lanes)).reshape(shape)

    spot = pl.ds(pl.multiple_of(me * width, width), width)

    def own(i, carry):
        pressure[i] = combine(p0[i + HALO, spot, :], u0[i + HALO, spot, :])
        return carry

    lax.fori_loop(0, layers, own, 0, unroll=4)
    ends = edges((rows, lanes))

    def halves(flow):
        out = jnp.maximum(flow, 0.0) + diffuse
        return out, out - flow

    def advance(i, carry):
        here, low_flow = carry
        above = combine(p0[i + HALO], u0[i + HALO])
        conc = wide[i + 1]
        high_flow = kz[i + 1] * (here - above)
        p_low, n_low = halves(low_flow)
        p_high, n_high = halves(high_flow)
        leave = p_high + n_low + rate[i]
        weights = [p_low, n_high]
        moved = p_low * wide[i] + n_high * wide[i + 2]
        for axis, face in ((0, kx), (1, ky)):
            at_low, at_high = ends[axis]
            flow = face[i + 1] * (here - following(here, axis))
            p_high, n_high = halves(flow)
            p_low, n_low = halves(preceding(flow, axis))
            leave = leave + (p_high + n_low)
            n_high = jnp.where(at_high, 0.0, n_high)
            p_low = jnp.where(at_low, 0.0, p_low)
            weights += [p_low, n_high]
            moved = moved + p_low * preceding(conc, axis) + n_high * following(conc, axis)
        stay = 1.0 - leave
        valid = jnp.where(i == 0, has_low, jnp.where(i == layers + 1, has_high, 1.0))
        first[i] = (stay * conc + moved) * valid
        slot = lax.rem(i, 2)
        for ref, weight in zip(coef, [stay] + weights):
            ref[slot] = weight
        return above, high_flow

    start = combine(p0[TSTEPS], u0[TSTEPS])
    carry = (start, kz[0] * (combine(p0[1], u0[1]) - start))
    carry = lax.fori_loop(0, 2, advance, carry)

    def body(i, carry):
        here = first[i - 1]
        slot = lax.rem(i - 1, 2)
        old = [ref[slot] for ref in coef]
        carry = advance(i, carry)
        stay, z_low, z_high, x_low, x_high, y_low, y_high = old
        result = stay * here + z_low * first[i - 2] + z_high * first[i]
        result = result + x_low * preceding(here, 0) + x_high * following(here, 0)
        free_out[i - 2] = result + y_low * preceding(here, 1) + y_high * following(here, 1)
        bound_out[i - 2] = bound[i - 2] + rate[i - 1] * (wide[i] + here)
        return carry

    lax.fori_loop(2, layers + 2, body, carry)


def shifts(array, axis):
    count = lax.axis_size(axis)
    moved = []
    for k in range(1, count):
        moved.append(lax.ppermute(array, axis, [(i, (i + k) % count) for i in range(count)]))
    return moved


def across(low, high):
    count = lax.axis_size("gz")
    from_low = lax.ppermute(high, "gz", [(i, i + 1) for i in range(count - 1)])
    from_high = lax.ppermute(low, "gz", [(i + 1, i) for i in range(count - 1)])
    return from_low, from_high


def total_over(array, axis):
    count = lax.axis_size(axis)
    step = 1
    while True:
        other = lax.ppermute(array, axis, [(i, i ^ step) for i in range(count)])
        step *= 2
        if step == count:
            return array, other
        array = array + other


def smem():
    return pl.BlockSpec(memory_space=pltpu.SMEM)


def vmem():
    return pl.BlockSpec(memory_space=pltpu.VMEM)


def f32(*shape):
    return jax.ShapeDtypeStruct(shape, jnp.float32)


def call(kernel, outs, scalars, arrays, scratch=(), aliases={}):
    size = sum(4 * math.prod(a.shape) for a in list(outs) + list(arrays) + list(scratch))
    return pl.pallas_call(
        kernel,
        out_shape=tuple(outs),
        in_specs=[smem()] * len(scalars) + [vmem()] * len(arrays),
        out_specs=(vmem(),) * len(outs),
        scratch_shapes=[pltpu.VMEM(s.shape, s.dtype) for s in scratch],
        input_output_aliases=aliases,
        compiler_params=pltpu.CompilerParams(vmem_limit_bytes=size + (4 << 20)),
    )(*scalars, *arrays)


def program(tissue, vessel_pressure, cond_table, leak_table, bind_table, hindrance, diffusivity, free_conc, bound_conc):
    layers, width, lanes = vessel_pressure.shape
    rows = tissue.shape[1]
    parts = rows // width
    rim = max(HALO, layers // 4)
    conc, bound = free_conc[0], bound_conc[0]
    rims = jnp.concatenate([vessel_pressure[:rim], vessel_pressure[layers - rim :]], 0)
    outer = shifts(rims, "size")
    inner = shifts(vessel_pressure[rim : layers - rim], "size")
    blocks = [rims] + outer

    def payload(pieces, labels, cells):
        arrays = pieces + [labels.astype(jnp.float32), cells]
        return jnp.concatenate([a.reshape(-1, lanes) for a in arrays], 0)

    low = payload([b[:HALO] for b in blocks], tissue[:HALO], conc[:TSTEPS])
    high = payload([b[2 * rim - HALO :] for b in blocks], tissue[layers - HALO :], conc[layers - TSTEPS :])
    from_low, from_high = across(low, high)
    extended = f32(layers + 2 * HALO, rows, lanes)
    stepped = f32(layers + 2, rows, lanes)
    faces = f32(layers + TSTEPS + 1, rows, lanes)
    p0, scaled, u0, cond, part, kx, ky, kz, rate, wide = call(
        functools.partial(rim_kernel, parts, rim),
        [extended] * 4 + [f32(4, 8, lanes), faces, faces, faces, stepped, f32(layers + 2 * TSTEPS, rows, lanes)],
        [cond_table, leak_table, bind_table, hindrance],
        [vessel_pressure, *outer, from_low, from_high, tissue, conc],
    )
    p0, scaled, u0, sums = call(
        functools.partial(core_kernel, parts, rim),
        [extended] * 3 + [f32(8, lanes)],
        [cond_table, leak_table],
        [vessel_pressure, *inner, tissue, cond, part, p0, scaled, u0],
        aliases={2 + parts + 3 + i: i for i in range(3)},
    )
    mine, theirs = total_over(sums, "gz")
    slab = f32(layers, rows, lanes)
    pressure, free, bound = call(
        functools.partial(transport_kernel, width),
        [f32(layers, width, lanes), slab, slab],
        [diffusivity],
        [mine, theirs, p0, u0, kx, ky, kz, rate, wide, bound],
        scratch=[stepped] + [f32(2, rows, lanes)] * 7,
    )
    return pressure, free[None], bound[None]


def solution(mesh):
    return jax.shard_map(
        program,
        mesh=mesh,
        in_specs=(
            P("gz", None, None),
            P("gz", "size", None),
            P(),
            P(),
            P("size", None),
            P("size"),
            P("size"),
            P("size", "gz", None, None),
            P("size", "gz", None, None),
        ),
        out_specs=(P("gz", "size", None), P("size", "gz", None, None), P("size", "gz", None, None)),
        check_vma=False,
    )
```

```python
import functools
import math
import jax
import jax.numpy as jnp
from jax import lax
from jax.experimental import pallas as pl
from jax.experimental.pallas import tpu as pltpu
from jax.sharding import PartitionSpec as P

TSTEPS = 2
HALO = TSTEPS + 1
DT = 0.1


def select(labels, values):
    return jnp.where(labels == 0, values[0], jnp.where(labels == 1, values[1], values[2]))


def following(cells, axis):
    return pltpu.roll(cells, cells.shape[axis] - 1, axis)


def preceding(cells, axis):
    return pltpu.roll(cells, 1, axis)


def edges(shape):
    row = lax.broadcasted_iota(jnp.int32, shape, 0)
    lane = lax.broadcasted_iota(jnp.int32, shape, 1)
    return (row == 0, row == shape[0] - 1), (lane == 0, lane == shape[1] - 1)


def inside():
    slab = lax.axis_index("gz")
    has_low = (slab > 0).astype(jnp.float32)
    has_high = (slab < lax.axis_size("gz") - 1).astype(jnp.float32)
    return has_low, has_high


def image(e, faces, inverse, p0, u0):
    kx, ky, kz = faces
    p = p0[e]
    pull = kz[e] * p0[e + 1] + kz[e - 1] * p0[e - 1]
    for axis, face in ((0, kx[e]), (1, ky[e])):
        pull = pull + (face * following(p, axis) + preceding(face * p, axis))
    u = p - inverse[e] * pull
    u0[e] = u
    return u


def products(e, u, u_next, totals, faces, diag, p0):
    kx, ky, kz = faces
    p = p0[e]
    d = diag[e - HALO]
    dp, du = d * p, d * u
    pull = kz[e] * u_next + kx[e] * following(u, 0) + ky[e] * following(u, 1)
    terms = (dp * p, dp * u, du * u, pull * u)
    return tuple(a + t.reshape(-1, 8, t.shape[-1]).sum(0) for a, t in zip(totals, terms))


def split_kernel(rim, vp, rims, inner):
    layers = vp.shape[0]
    rims[:rim] = vp[:rim]
    rims[rim:] = vp[layers - rim :]
    inner[...] = vp[rim : layers - rim]


def border_kernel(tissue, conc, low, high):
    layers, rows, _ = tissue.shape
    for j in range(HALO):
        low[j * rows : (j + 1) * rows, :] = tissue[j].astype(jnp.float32)
        high[j * rows : (j + 1) * rows, :] = tissue[layers - HALO + j].astype(jnp.float32)
    for j in range(TSTEPS):
        at = (HALO + j) * rows
        low[at : at + rows, :] = conc[j]
        high[at : at + rows, :] = conc[layers - TSTEPS + j]


def constants(cond_t, leak_t):
    cond_v = [cond_t[i] for i in range(3)]
    leak_v = [leak_t[i] for i in range(3)]
    diag_v = [6.0 * c * c + k for c, k in zip(cond_v, leak_v)]
    inverse_v = [1.0 / d for d in diag_v]
    ratio_v = [k / d for k, d in zip(leak_v, diag_v)]
    return cond_v, diag_v, inverse_v, ratio_v


def level(e, c, ends, kx, ky):
    kx[e] = jnp.where(ends[0][1], 0.0, c * following(c, 0))
    ky[e] = jnp.where(ends[1][1], 0.0, c * following(c, 1))


def prepare_kernel(cond_t, leak_t, bind_t, tissue, conc, kx, ky, kz, diag, inverse, ratio, rate, wide):
    layers, _, _ = tissue.shape
    cond_v, diag_v, inverse_v, ratio_v = constants(cond_t, leak_t)
    rate_v = [bind_t[0, i] * DT for i in range(3)]
    ends = edges(tissue.shape[1:])

    def own(i, before):
        e = i + HALO
        labels = tissue[i]
        c = select(labels, cond_v)
        diag[i] = select(labels, diag_v)
        inverse[e] = select(labels, inverse_v)
        ratio[i] = select(labels, ratio_v)
        rate[e] = select(labels, rate_v)
        wide[i + TSTEPS] = conc[i]
        level(e, c, ends, kx, ky)
        kz[e - 1] = before * c
        return c

    lax.fori_loop(0, layers, own, jnp.zeros(tissue.shape[1:], jnp.float32), unroll=2)


def rim_kernel(parts, rim, width, cond_t, leak_t, bind_t, *refs):
    blocks, refs = refs[0], refs[1:]
    from_low, from_high, tissue, diag, ratio = refs[:5]
    kx, ky, kz, inverse, rate, p0, u0, sums = refs[10:]
    layers, rows, _ = tissue.shape
    me = lax.axis_index("size")
    has_low, has_high = inside()
    cond_v, _, inverse_v, ratio_v = constants(cond_t, leak_t)
    rate_v = [bind_t[0, i] * DT for i in range(3)]
    tis_at = parts * HALO * width
    ends = edges(tissue.shape[1:])

    def halo(side, j, e, valid):
        at = tis_at + j * rows
        labels = side[at : at + rows, :]
        c = select(labels, cond_v) * valid
        level(e, c, ends, kx, ky)
        inverse[e] = select(labels, inverse_v)
        rate[e] = select(labels, rate_v)
        return c

    low = [halo(from_low, j, j, has_low) for j in range(HALO)] + [select(tissue[0], cond_v)]
    high = [select(tissue[layers - 1], cond_v)] + [halo(from_high, j, layers + HALO + j, has_high) for j in range(HALO)]
    for j in range(HALO):
        kz[j] = low[j] * low[j + 1]
        kz[layers + HALO - 1 + j] = high[j] * high[j + 1]

    for k in range(parts):
        column = pl.multiple_of((me ^ k) * width, width)
        spot = pl.ds(column, width)
        base = k * 2 * rim

        def fill(i, carry):
            high = i + (layers - rim)
            p0[i + HALO, spot, :] = blocks[i + base] * ratio[i, spot, :]
            p0[high + HALO, spot, :] = blocks[i + (base + rim)] * ratio[high, spot, :]
            return carry

        lax.fori_loop(0, rim, fill, 0)
        for j in range(HALO):
            at = (k * HALO + j) * width
            for side, e in ((from_low, j), (from_high, layers + HALO + j)):
                labels = side[pl.ds(pl.multiple_of(tis_at + j * rows + column, width), width), :]
                p0[e, spot, :] = side[at : at + width, :] * select(labels, ratio_v)

    faces = (kx, ky, kz)

    def both(e, carry):
        image(e, faces, inverse, p0, u0)
        image(layers + 2 * HALO - 1 - e, faces, inverse, p0, u0)
        return carry

    lax.fori_loop(1, rim + HALO - 1, both, 0)

    def sum_over(first, count, totals):
        def body(i, carry):
            e = i + HALO
            return products(e, u0[e], u0[e + 1], carry, faces, diag, p0)

        return lax.fori_loop(first, first + count, body, totals)

    zero = jnp.zeros((8, tissue.shape[2]), jnp.float32)
    totals = sum_over(0, rim - 2, (zero,) * 4)
    totals = sum_over(layers - rim + 1, rim - 1, totals)
    for i in range(4):
        sums[i] = totals[i]


def core_kernel(parts, rim, vp, *refs):
    inner = refs[: parts - 1]
    refs = refs[parts - 1 :]
    kx, ky, kz, diag, inverse, ratio, part, from_low, from_high = refs[:9]
    p0, u0, wide, sums = refs[12:]
    rows = wide.shape[1]
    for j in range(TSTEPS):
        at = from_low.shape[0] - (TSTEPS - j) * rows
        wide[j] = from_low[at : at + rows, :]
        wide[wide.shape[0] - TSTEPS + j] = from_high[at : at + rows, :]
    layers, width, _ = vp.shape
    me = lax.axis_index("size")
    for k in range(parts):
        spot = pl.ds(pl.multiple_of((me ^ k) * width, width), width)
        source = vp if k == 0 else inner[k - 1]
        start = rim if k == 0 else 0

        def fill(i, carry):
            p0[i + (rim + HALO), spot, :] = source[i + start] * ratio[i + rim, spot, :]
            return carry

        lax.fori_loop(0, layers - 2 * rim, fill, 0, unroll=2)
    faces = (kx, ky, kz)
    first = rim + HALO - 1
    last = layers - rim + HALO

    def body(e, carry):
        before, totals = carry
        here = image(e, faces, inverse, p0, u0)
        return here, products(e - 1, before, here, totals, faces, diag, p0)

    totals = tuple(part[i] for i in range(4))
    before, totals = lax.fori_loop(first, last + 1, body, (u0[first - 1], totals))
    totals = products(last, before, u0[last + 1], totals, faces, diag, p0)
    sums[...] = jnp.concatenate([t.sum(0, keepdims=True) for t in totals] * 2, 0)


def transport_kernel(width, hinder_t, diffuse_t, mine, theirs, p0, u0, kx, ky, kz, rate, wide, bound, pressure, free_out, bound_out, first, *coef):
    layers, rows, lanes = bound.shape
    me = lax.axis_index("size")
    has_low, has_high = inside()
    sums = mine[...] + theirs[...]
    rho, drop, second, shared = [jnp.sum(sums[i : i + 1, :], axis=1, keepdims=True) for i in range(4)]
    third = second - 2.0 * shared
    alpha = rho / drop
    rho_next = alpha * alpha * second - rho
    beta = rho_next / rho
    curve = drop - 2.0 * alpha * second + alpha * alpha * third - beta * rho_next / alpha
    alpha_next = rho_next / curve
    on_p = jnp.broadcast_to(alpha + alpha_next * (1.0 + beta), (8, lanes))[None]
    on_u = jnp.broadcast_to(-alpha_next * alpha, (8, lanes))[None]
    diffuse = diffuse_t[0] * DT
    hinder = hinder_t[0] * DT

    def combine(p, u, by_p, by_u):
        return (by_p * p.reshape(-1, 8, lanes) + by_u * u.reshape(-1, 8, lanes)).reshape(p.shape)

    spot = pl.ds(pl.multiple_of(me * width, width), width)

    def own(i, carry):
        pressure[i] = combine(p0[i + HALO, spot, :], u0[i + HALO, spot, :], on_p, on_u)
        return carry

    lax.fori_loop(0, layers, own, 0, unroll=4)
    drive_p, drive_u = hinder * on_p, hinder * on_u
    ends = edges((rows, lanes))

    def drive(e):
        return combine(p0[e], u0[e], drive_p, drive_u)

    def halves(flow):
        out = jnp.maximum(flow, 0.0) + diffuse
        return out, out - flow

    def advance(i, carry):
        here, low_flow = carry
        e = i + TSTEPS
        above = drive(e + 1)
        conc = wide[i + 1]
        high_flow = kz[e] * (here - above)
        p_low, n_low = halves(low_flow)
        p_high, n_high = halves(high_flow)
        leave = p_high + n_low + rate[e]
        weights = [p_low, n_high]
        moved = p_low * wide[i] + n_high * wide[i + 2]
        for axis, face in ((0, kx), (1, ky)):
            at_low, at_high = ends[axis]
            flow = face[e] * (here - following(here, axis))
            p_high, n_high = halves(flow)
            p_low, n_low = halves(preceding(flow, axis))
            leave = leave + (p_high + n_low)
            n_high = jnp.where(at_high, 0.0, n_high)
            p_low = jnp.where(at_low, 0.0, p_low)
            weights += [p_low, n_high]
            moved = moved + p_low * preceding(conc, axis) + n_high * following(conc, axis)
        stay = 1.0 - leave
        valid = jnp.where(i == 0, has_low, jnp.where(i == layers + 1, has_high, 1.0))
        first[i] = (stay * conc + moved) * valid
        slot = lax.rem(i, 2)
        for ref, weight in zip(coef, [stay] + weights):
            ref[slot] = weight
        return above, high_flow

    start = drive(TSTEPS)
    carry = (start, kz[TSTEPS - 1] * (drive(TSTEPS - 1) - start))
    carry = lax.fori_loop(0, 2, advance, carry)

    def body(i, carry):
        here = first[i - 1]
        slot = lax.rem(i - 1, 2)
        old = [ref[slot] for ref in coef]
        carry = advance(i, carry)
        stay, z_low, z_high, x_low, x_high, y_low, y_high = old
        result = stay * here + z_low * first[i - 2] + z_high * first[i]
        result = result + x_low * preceding(here, 0) + x_high * following(here, 0)
        free_out[i - 2] = result + y_low * preceding(here, 1) + y_high * following(here, 1)
        bound_out[i - 2] = bound[i - 2] + rate[i + 1] * (wide[i] + here)
        return carry

    lax.fori_loop(2, layers + 2, body, carry)


def swapped(array, axis, bit):
    count = lax.axis_size(axis)
    return lax.ppermute(array, axis, [(i, i ^ bit) for i in range(count)])


def butterfly(array, axis):
    bit = 1
    while bit < lax.axis_size(axis):
        array = jnp.concatenate([array, swapped(array, axis, bit)], 0)
        bit *= 2
    return array


def across(low, high):
    count = lax.axis_size("gz")
    from_low = lax.ppermute(high, "gz", [(i, i + 1) for i in range(count - 1)])
    from_high = lax.ppermute(low, "gz", [(i + 1, i) for i in range(count - 1)])
    return from_low, from_high


def total_over(array, axis):
    count = lax.axis_size(axis)
    step = 1
    while True:
        other = lax.ppermute(array, axis, [(i, i ^ step) for i in range(count)])
        step *= 2
        if step == count:
            return array, other
        array = array + other


def smem():
    return pl.BlockSpec(memory_space=pltpu.SMEM)


def vmem():
    return pl.BlockSpec(memory_space=pltpu.VMEM)


def f32(*shape):
    return jax.ShapeDtypeStruct(shape, jnp.float32)


def call(kernel, outs, scalars, arrays, scratch=(), aliases={}):
    size = sum(4 * math.prod(a.shape) for a in list(outs) + list(arrays) + list(scratch))
    return pl.pallas_call(
        kernel,
        out_shape=tuple(outs),
        in_specs=[smem()] * len(scalars) + [vmem()] * len(arrays),
        out_specs=(vmem(),) * len(outs),
        scratch_shapes=[pltpu.VMEM(s.shape, s.dtype) for s in scratch],
        input_output_aliases=aliases,
        compiler_params=pltpu.CompilerParams(vmem_limit_bytes=size + (4 << 20)),
    )(*scalars, *arrays)


def program(tissue, vessel_pressure, cond_table, leak_table, bind_table, hindrance, diffusivity, free_conc, bound_conc):
    layers, width, lanes = vessel_pressure.shape
    rows = tissue.shape[1]
    parts = rows // width
    rim = HALO
    conc, bound = free_conc[0], bound_conc[0]
    slab = f32(layers, rows, lanes)
    extended = f32(layers + 2 * HALO, rows, lanes)
    wider = f32(layers + 2 * TSTEPS, rows, lanes)
    rims, middle = call(
        functools.partial(split_kernel, rim),
        [f32(2 * rim, width, lanes), f32(layers - 2 * rim, width, lanes)],
        [],
        [vessel_pressure],
    )
    blocks = butterfly(rims, "size")
    inner = [swapped(middle, "size", k) for k in range(1, parts)]
    border = f32((HALO + TSTEPS) * rows, lanes)
    border_low, border_high = call(border_kernel, [border] * 2, [], [tissue, conc])

    def payload(first, border):
        pieces = [blocks[k * 2 * rim + first : k * 2 * rim + first + HALO] for k in range(parts)] + [border]
        return jnp.concatenate([a.reshape(-1, lanes) for a in pieces], 0)

    from_low, from_high = across(payload(0, border_low), payload(2 * rim - HALO, border_high))
    kx, ky, kz, diag, inverse, ratio, rate, wide = call(
        prepare_kernel,
        [extended] * 3 + [slab, extended, slab, extended, wider],
        [cond_table, leak_table, bind_table],
        [tissue, conc],
    )
    kx, ky, kz, inverse, rate, p0, u0, part = call(
        functools.partial(rim_kernel, parts, rim, width),
        [extended] * 7 + [f32(4, 8, lanes)],
        [cond_table, leak_table, bind_table],
        [blocks, from_low, from_high, tissue, diag, ratio, kx, ky, kz, inverse, rate],
        aliases={9 + i: i for i in range(5)},
    )
    p0, u0, wide, sums = call(
        functools.partial(core_kernel, parts, rim),
        [extended] * 2 + [wider, f32(8, lanes)],
        [],
        [vessel_pressure, *inner, kx, ky, kz, diag, inverse, ratio, part, from_low, from_high, p0, u0, wide],
        aliases={parts + 9 + i: i for i in range(3)},
    )
    mine, theirs = total_over(sums, "gz")
    pressure, free, bound = call(
        functools.partial(transport_kernel, width),
        [f32(layers, width, lanes), slab, slab],
        [hindrance, diffusivity],
        [mine, theirs, p0, u0, kx, ky, kz, rate, wide, bound],
        scratch=[f32(layers + 2, rows, lanes)] + [f32(2, rows, lanes)] * 7,
    )
    return pressure, free[None], bound[None]


def solution(mesh):
    return jax.shard_map(
        program,
        mesh=mesh,
        in_specs=(
            P("gz", None, None),
            P("gz", "size", None),
            P(),
            P(),
            P("size", None),
            P("size"),
            P("size"),
            P("size", "gz", None, None),
            P("size", "gz", None, None),
        ),
        out_specs=(P("gz", "size", None), P("size", "gz", None, None), P("size", "gz", None, None)),
        check_vma=False,
    )
```

```python
import functools
import math
import jax
import jax.numpy as jnp
from jax import lax
from jax.experimental import pallas as pl
from jax.experimental.pallas import tpu as pltpu
from jax.sharding import PartitionSpec as P

TSTEPS = 2
HALO = TSTEPS + 1
DT = 0.1


def select(labels, values):
    return jnp.where(labels == 0, values[0], jnp.where(labels == 1, values[1], values[2]))


def following(cells, axis):
    return pltpu.roll(cells, cells.shape[axis] - 1, axis)


def preceding(cells, axis):
    return pltpu.roll(cells, 1, axis)


def edges(shape):
    row = lax.broadcasted_iota(jnp.int32, shape, 0)
    lane = lax.broadcasted_iota(jnp.int32, shape, 1)
    return (row == 0, row == shape[0] - 1), (lane == 0, lane == shape[1] - 1)


def inside():
    slab = lax.axis_index("gz")
    has_low = (slab > 0).astype(jnp.float32)
    has_high = (slab < lax.axis_size("gz") - 1).astype(jnp.float32)
    return has_low, has_high


def at(ref, layer, rows, shift=0):
    if shift == 0:
        return ref[pl.ds(pl.multiple_of(layer * rows, 8), rows), :]
    view = ref.at[pl.ds(pl.multiple_of(layer * rows - 8, 8), rows + 16), :]
    return view[8 + shift : 8 + shift + rows, :]


def put(ref, layer, value):
    rows = value.shape[0]
    ref[pl.ds(pl.multiple_of(layer * rows, 8), rows), :] = value


def image(e, rows, faces, inverse, p0, u0, p_next):
    kx, ky, kz = faces
    p, y = at(p0, e, rows), at(ky, e, rows)
    ahead = following(p, 1)
    pull = at(kz, e, rows) * at(p0, e + 1, rows) + at(kz, e - 1, rows) * at(p0, e - 1, rows)
    pull = pull + (at(kx, e, rows) * at(p0, e, rows, 1) + at(kx, e, rows, -1) * at(p0, e, rows, -1))
    pull = pull + (y * ahead + preceding(y * p, 1))
    put(p_next, e, ahead)
    put(u0, e, p - at(inverse, e, rows) * pull)


def products(e, rows, totals, faces, diag, p0, u0, u_next):
    kx, ky, kz = faces
    p, u = at(p0, e, rows), at(u0, e, rows)
    d = at(diag, e - HALO, rows)
    dp, du = d * p, d * u
    ahead = following(u, 1)
    pull = at(kz, e, rows) * at(u0, e + 1, rows) + at(kx, e, rows) * at(u0, e, rows, 1) + at(ky, e, rows) * ahead
    put(u_next, e, ahead)
    terms = (dp * p, dp * u, du * u, pull * u)
    return tuple(a + t.reshape(-1, 8, t.shape[-1]).sum(0) for a, t in zip(totals, terms))


def split_kernel(rim, vp, rims, inner):
    layers = vp.shape[0]
    rims[:rim] = vp[:rim]
    rims[rim:] = vp[layers - rim :]
    inner[...] = vp[rim : layers - rim]


def border_kernel(tissue, conc, low, high):
    layers, rows, _ = tissue.shape
    for j in range(HALO):
        low[j * rows : (j + 1) * rows, :] = tissue[j].astype(jnp.float32)
        high[j * rows : (j + 1) * rows, :] = tissue[layers - HALO + j].astype(jnp.float32)
    for j in range(TSTEPS):
        at = (HALO + j) * rows
        low[at : at + rows, :] = conc[j]
        high[at : at + rows, :] = conc[layers - TSTEPS + j]


def constants(cond_t, leak_t):
    cond_v = [cond_t[i] for i in range(3)]
    leak_v = [leak_t[i] for i in range(3)]
    diag_v = [6.0 * c * c + k for c, k in zip(cond_v, leak_v)]
    inverse_v = [1.0 / d for d in diag_v]
    ratio_v = [k / d for k, d in zip(leak_v, diag_v)]
    return cond_v, diag_v, inverse_v, ratio_v


def level(e, c, ends, kx, ky):
    put(kx, e, jnp.where(ends[0][1], 0.0, c * following(c, 0)))
    put(ky, e, jnp.where(ends[1][1], 0.0, c * following(c, 1)))


def remaining(rate, diffuse, ends):
    stay = 1.0 - rate
    for low, high in ends:
        stay = stay - jnp.where(low, diffuse, 0.0) - jnp.where(high, diffuse, 0.0)
    return stay


def prepare_kernel(rows, cond_t, leak_t, bind_t, diffuse_t, tissue, conc, kx, ky, kz, diag, inverse, ratio, rate, keep, wide):
    shape = (rows, tissue.shape[1])
    layers = tissue.shape[0] // rows
    cond_v, diag_v, inverse_v, ratio_v = constants(cond_t, leak_t)
    rate_v = [bind_t[0, i] * DT for i in range(3)]
    ends = edges(shape)
    base = remaining(0.0, diffuse_t[0] * DT, ends)

    def own(i, before):
        e = i + HALO
        labels = at(tissue, i, rows)
        c = select(labels, cond_v)
        r = select(labels, rate_v)
        put(diag, i, select(labels, diag_v))
        put(inverse, e, select(labels, inverse_v))
        put(ratio, i, select(labels, ratio_v))
        put(rate, i, r)
        put(keep, i + 1, base - r)
        put(wide, i + TSTEPS, at(conc, i, rows))
        level(e, c, ends, kx, ky)
        put(kz, e - 1, before * c)
        return c

    lax.fori_loop(0, layers, own, jnp.zeros(shape, jnp.float32), unroll=2)


def rim_kernel(parts, rim, width, rows, cond_t, leak_t, bind_t, diffuse_t, blocks, from_low, from_high, tissue, diag, ratio, *refs):
    kx, ky, kz, inverse, keep, wide, p0, u0, p_next, u_next, sums = refs[6:]
    lanes = tissue.shape[1]
    layers = tissue.shape[0] // rows
    me = lax.axis_index("size")
    has_low, has_high = inside()
    cond_v, _, inverse_v, ratio_v = constants(cond_t, leak_t)
    rate_v = [bind_t[0, i] * DT for i in range(3)]
    tis_at = parts * HALO * width
    conc_at = tis_at + HALO * rows
    ends = edges((rows, lanes))

    def labels_of(side, j):
        return side[tis_at + j * rows : tis_at + (j + 1) * rows, :]

    def halo(side, j, e, valid):
        labels = labels_of(side, j)
        c = select(labels, cond_v) * valid
        level(e, c, ends, kx, ky)
        put(inverse, e, select(labels, inverse_v))
        return c

    low = [halo(from_low, j, j, has_low) for j in range(HALO)] + [select(at(tissue, 0, rows), cond_v)]
    high = [select(at(tissue, layers - 1, rows), cond_v)] + [halo(from_high, j, layers + HALO + j, has_high) for j in range(HALO)]
    for j in range(HALO):
        put(kz, j, low[j] * low[j + 1])
        put(kz, layers + HALO - 1 + j, high[j] * high[j + 1])
    for side, j, layer in ((from_low, HALO - 1, 0), (from_high, 0, layers + 1)):
        put(keep, layer, remaining(select(labels_of(side, j), rate_v), diffuse_t[0] * DT, ends))
    for j in range(TSTEPS):
        span = slice(conc_at + j * rows, conc_at + (j + 1) * rows)
        put(wide, j, from_low[span, :])
        put(wide, layers + TSTEPS + j, from_high[span, :])

    for k in range(parts):
        column = pl.multiple_of((me ^ k) * width, width)

        def spot(layer):
            return pl.ds(pl.multiple_of(layer * rows + column, width), width)

        for i in range(rim):
            top = i + (layers - rim)
            p0[spot(i + HALO), :] = blocks[k * 2 * rim + i] * ratio[spot(i), :]
            p0[spot(top + HALO), :] = blocks[k * 2 * rim + rim + i] * ratio[spot(top), :]
        for j in range(HALO):
            span = slice((k * HALO + j) * width, (k * HALO + j + 1) * width)
            for side, e in ((from_low, j), (from_high, layers + HALO + j)):
                labels = side[pl.ds(pl.multiple_of(tis_at + j * rows + column, width), width), :]
                p0[spot(e), :] = side[span, :] * select(labels, ratio_v)

    faces = (kx, ky, kz)

    def both(e, carry):
        image(e, rows, faces, inverse, p0, u0, p_next)
        image(layers + 2 * HALO - 1 - e, rows, faces, inverse, p0, u0, p_next)
        return carry

    lax.fori_loop(1, rim + HALO - 1, both, 0)
    for e in (HALO - 1, layers + HALO):
        put(u_next, e, following(at(u0, e, rows), 1))

    def sum_over(first, count, totals):
        def body(i, carry):
            return products(i + HALO, rows, carry, faces, diag, p0, u0, u_next)

        return lax.fori_loop(first, first + count, body, totals)

    zero = jnp.zeros((8, lanes), jnp.float32)
    totals = sum_over(0, rim - 2, (zero,) * 4)
    totals = sum_over(layers - rim + 1, rim - 1, totals)
    for i in range(4):
        sums[i] = totals[i]


def core_kernel(parts, rim, rows, vp, *refs):
    inner = refs[: parts - 1]
    refs = refs[parts - 1 :]
    kx, ky, kz, diag, inverse, ratio, part = refs[:7]
    p0, u0, p_next, u_next, sums = refs[11:]
    layers, width, _ = vp.shape
    me = lax.axis_index("size")
    for k in range(parts):
        column = pl.multiple_of((me ^ k) * width, width)
        source = vp if k == 0 else inner[k - 1]
        start = rim if k == 0 else 0

        def spot(layer):
            return pl.ds(pl.multiple_of(layer * rows + column, width), width)

        for i in range(layers - 2 * rim):
            p0[spot(i + (rim + HALO)), :] = source[i + start] * ratio[spot(i + rim), :]

    faces = (kx, ky, kz)
    first = rim + HALO - 1
    last = layers - rim + HALO

    def terms(e, totals):
        return products(e, rows, totals, faces, diag, p0, u0, u_next)

    def picture(e):
        image(e, rows, faces, inverse, p0, u0, p_next)

    def body(i, totals):
        e = first + 2 * i
        totals = terms(e - 2, terms(e - 3, totals))
        picture(e)
        picture(e + 1)
        return totals

    picture(first)
    picture(first + 1)
    pairs = (last + 1 - first) // 2
    totals = lax.fori_loop(1, pairs, body, tuple(part[i] for i in range(4)))
    done = first + 2 * pairs
    for e in range(done, last + 1):
        picture(e)
    for e in range(done - 3, last + 1):
        totals = terms(e, totals)
    sums[...] = jnp.concatenate([t.sum(0, keepdims=True) for t in totals] * 2, 0)


def slide_kernel(rows, wide, low, high):
    def body(i, carry):
        conc = at(wide, i + 1, rows)
        put(low, i, preceding(conc, 1))
        put(high, i, following(conc, 1))
        return carry

    lax.fori_loop(0, low.shape[0] // rows, body, 0, unroll=2)


def transport_kernel(width, rows, hinder_t, diffuse_t, mine, theirs, p0, u0, p_next, u_next, kx, ky, kz, rate, keep, wide, wide_low, wide_high, bound, pressure, free_out, bound_out, press, first, kept, zo, zb, xo, xb, yo, yb):
    lanes = bound.shape[1]
    layers = bound.shape[0] // rows
    me = lax.axis_index("size")
    has_low, has_high = inside()
    sums = mine[...] + theirs[...]
    rho, drop, second, shared = [jnp.sum(sums[i : i + 1, :], axis=1, keepdims=True) for i in range(4)]
    third = second - 2.0 * shared
    alpha = rho / drop
    rho_next = alpha * alpha * second - rho
    beta = rho_next / rho
    curve = drop - 2.0 * alpha * second + alpha * alpha * third - beta * rho_next / alpha
    alpha_next = rho_next / curve
    on_p = jnp.broadcast_to(alpha + alpha_next * (1.0 + beta), (8, lanes))[None]
    on_u = jnp.broadcast_to(-alpha_next * alpha, (8, lanes))[None]
    diffuse = diffuse_t[0] * DT
    hinder = hinder_t[0] * DT

    def combine(p, u, by_p, by_u):
        return (by_p * p.reshape(-1, 8, lanes) + by_u * u.reshape(-1, 8, lanes)).reshape(p.shape)

    def own(i, carry):
        spot = pl.ds(pl.multiple_of((i + HALO) * rows + me * width, width), width)
        put(pressure, i, combine(p0[spot, :], u0[spot, :], on_p, on_u))
        return carry

    lax.fori_loop(0, layers, own, 0, unroll=8)
    drive_p, drive_u = hinder * on_p, hinder * on_u

    def halves(flow, through):
        out = jnp.maximum(flow, 0.0) + through
        return out, out - flow

    def near(ref, layer, shift=0):
        return at(ref, layer, rows, shift)

    def store(ref, layer, value):
        put(ref, layer, value)

    def drive(e):
        store(press, e, combine(near(p0, e), near(u0, e), drive_p, drive_u))

    lane = lax.broadcasted_iota(jnp.int32, (rows, lanes), 1)
    row = lax.broadcasted_iota(jnp.int32, (rows, lanes), 0)
    along = jnp.where(row == rows - 1, 0.0, diffuse)
    rising = jnp.where(lane == lanes - 1, 0.0, diffuse)
    falling = jnp.where(lane == 0, 0.0, diffuse)

    def advance(i):
        e = i + TSTEPS
        here, conc = near(press, e), near(wide, i + 1)
        z_out, z_back = near(zo, i), near(zb, i)
        z_up, z_down = halves(near(kz, e) * (here - near(press, e + 1)), diffuse)
        stay = near(keep, i) - z_up - z_back
        moved = z_out * near(wide, i) + z_down * near(wide, i + 2)
        out, back = halves(near(kx, e) * (here - near(press, e, 1)), along)
        into = preceding(out, 0)
        stay = stay - out - preceding(back, 0)
        moved = moved + into * near(wide, i + 1, -1) + back * near(wide, i + 1, 1)
        flow = near(ky, e) * (here - combine(near(p_next, e), near(u_next, e), drive_p, drive_u))
        out, y_back = halves(flow, rising)
        y_into, y_low = halves(preceding(flow, 1), falling)
        stay = stay - out - y_low
        moved = moved + y_into * near(wide_low, i) + y_back * near(wide_high, i)
        drive(e + 2)
        for ref, value in ((zo, z_up), (zb, z_down), (xo, into), (xb, back), (yo, y_into), (yb, y_back), (kept, stay)):
            store(ref, i + 1, value)
        valid = jnp.where(i == 0, has_low, jnp.where(i == layers + 1, has_high, 1.0))
        store(first, i + 1, (stay * conc + moved) * valid)

    def finish(i):
        here = near(first, i + 1)
        result = near(kept, i + 1) * here + near(zo, i) * near(first, i) + near(zb, i + 1) * near(first, i + 2)
        result = result + near(xo, i + 1) * near(first, i + 1, -1) + near(xb, i + 1) * near(first, i + 1, 1)
        result = result + near(yo, i + 1) * preceding(here, 1) + near(yb, i + 1) * following(here, 1)
        store(free_out, i - 1, result)
        gain = near(rate, i - 1) * (near(wide, i + 1) + here)
        store(bound_out, i - 1, near(bound, i - 1) + gain)

    for e in range(TSTEPS - 1, TSTEPS + 2):
        drive(e)
    z_out, z_back = halves(near(kz, TSTEPS - 1) * (near(press, TSTEPS - 1) - near(press, TSTEPS)), diffuse)
    store(zo, 0, z_out)
    store(zb, 0, z_back)

    def begin(i, carry):
        advance(i)
        return carry

    lax.fori_loop(0, 3, begin, 0)

    def body(i, carry):
        finish(i - 2)
        advance(i)
        return carry

    lax.fori_loop(3, layers + 2, body, 0)
    finish(layers)


def swapped(array, axis, bit):
    count = lax.axis_size(axis)
    return lax.ppermute(array, axis, [(i, i ^ bit) for i in range(count)])


def butterfly(array, axis):
    bit = 1
    while bit < lax.axis_size(axis):
        array = jnp.concatenate([array, swapped(array, axis, bit)], 0)
        bit *= 2
    return array


def across(low, high):
    count = lax.axis_size("gz")
    from_low = lax.ppermute(high, "gz", [(i, i + 1) for i in range(count - 1)])
    from_high = lax.ppermute(low, "gz", [(i + 1, i) for i in range(count - 1)])
    return from_low, from_high


def total_over(array, axis):
    count = lax.axis_size(axis)
    step = 1
    while True:
        other = swapped(array, axis, step)
        step *= 2
        if step == count:
            return array, other
        array = array + other


def smem():
    return pl.BlockSpec(memory_space=pltpu.SMEM)


def vmem():
    return pl.BlockSpec(memory_space=pltpu.VMEM)


def f32(*shape):
    return jax.ShapeDtypeStruct(shape, jnp.float32)


def call(kernel, outs, scalars, arrays, scratch=(), aliases={}):
    size = sum(4 * math.prod(a.shape) for a in list(outs) + list(arrays) + list(scratch))
    return pl.pallas_call(
        kernel,
        out_shape=tuple(outs),
        in_specs=[smem()] * len(scalars) + [vmem()] * len(arrays),
        out_specs=(vmem(),) * len(outs),
        scratch_shapes=[pltpu.VMEM(s.shape, s.dtype) for s in scratch],
        input_output_aliases=aliases,
        compiler_params=pltpu.CompilerParams(vmem_limit_bytes=size + (4 << 20)),
    )(*scalars, *arrays)


def program(tissue, vessel_pressure, cond_table, leak_table, bind_table, hindrance, diffusivity, free_conc, bound_conc):
    layers, width, lanes = vessel_pressure.shape
    rows = tissue.shape[1]
    parts = rows // width
    rim = HALO
    conc, bound = free_conc[0], bound_conc[0]
    slab = f32(layers * rows, lanes)
    extended = f32((layers + 2 * HALO) * rows, lanes)
    stepped = f32((layers + 2) * rows, lanes)
    wider = f32((layers + 2 * TSTEPS) * rows, lanes)
    rims, middle = call(
        functools.partial(split_kernel, rim),
        [f32(2 * rim, width, lanes), f32(layers - 2 * rim, width, lanes)],
        [],
        [vessel_pressure],
    )
    blocks = butterfly(rims, "size")
    inner = [swapped(middle, "size", k) for k in range(1, parts)]
    border = f32((HALO + TSTEPS) * rows, lanes)
    border_low, border_high = call(border_kernel, [border] * 2, [], [tissue, conc])

    def payload(first, border):
        pieces = [blocks[k * 2 * rim + first : k * 2 * rim + first + HALO] for k in range(parts)] + [border]
        return jnp.concatenate([a.reshape(-1, lanes) for a in pieces], 0)

    from_low, from_high = across(payload(0, border_low), payload(2 * rim - HALO, border_high))
    tissue, conc, bound = (a.reshape(-1, lanes) for a in (tissue, conc, bound))
    kx, ky, kz, diag, inverse, ratio, rate, keep, wide = call(
        functools.partial(prepare_kernel, rows),
        [extended] * 3 + [slab, extended, slab, slab, stepped, wider],
        [cond_table, leak_table, bind_table, diffusivity],
        [tissue, conc],
    )
    kx, ky, kz, inverse, keep, wide, p0, u0, p_next, u_next, part = call(
        functools.partial(rim_kernel, parts, rim, width, rows),
        [extended] * 4 + [stepped, wider] + [extended] * 4 + [f32(4, 8, lanes)],
        [cond_table, leak_table, bind_table, diffusivity],
        [blocks, from_low, from_high, tissue, diag, ratio, kx, ky, kz, inverse, keep, wide],
        aliases={10 + i: i for i in range(6)},
    )
    p0, u0, p_next, u_next, sums = call(
        functools.partial(core_kernel, parts, rim, rows),
        [extended] * 4 + [f32(8, lanes)],
        [],
        [vessel_pressure, *inner, kx, ky, kz, diag, inverse, ratio, part, p0, u0, p_next, u_next],
        aliases={parts + 7 + i: i for i in range(4)},
    )
    wide_low, wide_high = call(functools.partial(slide_kernel, rows), [stepped] * 2, [], [wide])
    mine, theirs = total_over(sums, "gz")
    pressure, free, bound = call(
        functools.partial(transport_kernel, width, rows),
        [f32(layers * width, lanes), slab, slab],
        [hindrance, diffusivity],
        [mine, theirs, p0, u0, p_next, u_next, kx, ky, kz, rate, keep, wide, wide_low, wide_high, bound],
        scratch=[f32((layers + 2 * HALO + 1) * rows, lanes)] + [wider] * 8,
    )
    shape = (1, layers, rows, lanes)
    return pressure.reshape(layers, width, lanes), free.reshape(shape), bound.reshape(shape)


def solution(mesh):
    return jax.shard_map(
        program,
        mesh=mesh,
        in_specs=(
            P("gz", None, None),
            P("gz", "size", None),
            P(),
            P(),
            P("size", None),
            P("size"),
            P("size"),
            P("size", "gz", None, None),
            P("size", "gz", None, None),
        ),
        out_specs=(P("gz", "size", None), P("size", "gz", None, None), P("size", "gz", None, None)),
        check_vma=False,
    )
```

```python
import functools
import math
import jax
import jax.numpy as jnp
from jax import lax
from jax.experimental import pallas as pl
from jax.experimental.pallas import tpu as pltpu
from jax.sharding import PartitionSpec as P

TSTEPS = 2
HALO = TSTEPS + 1
DT = 0.1
EARLY = 8


def select(labels, values):
    return jnp.where(labels == 0, values[0], jnp.where(labels == 1, values[1], values[2]))


def following(cells, axis):
    return pltpu.roll(cells, cells.shape[axis] - 1, axis)


def preceding(cells, axis):
    return pltpu.roll(cells, 1, axis)


def edges(shape):
    row = lax.broadcasted_iota(jnp.int32, shape, 0)
    lane = lax.broadcasted_iota(jnp.int32, shape, 1)
    return (row == 0, row == shape[0] - 1), (lane == 0, lane == shape[1] - 1)


def inside():
    slab = lax.axis_index("gz")
    has_low = (slab > 0).astype(jnp.float32)
    has_high = (slab < lax.axis_size("gz") - 1).astype(jnp.float32)
    return has_low, has_high


def at(ref, layer, rows, shift=0):
    if shift == 0:
        return ref[pl.ds(pl.multiple_of(layer * rows, 8), rows), :]
    view = ref.at[pl.ds(pl.multiple_of(layer * rows - 8, 8), rows + 16), :]
    return view[8 + shift : 8 + shift + rows, :]


def put(ref, layer, value):
    rows = value.shape[0]
    ref[pl.ds(pl.multiple_of(layer * rows, 8), rows), :] = value


def image(e, rows, faces, inverse, p0, u0, p_next):
    kx, ky, kz = faces
    p, y = at(p0, e, rows), at(ky, e, rows)
    ahead = following(p, 1)
    pull = at(kz, e, rows) * at(p0, e + 1, rows) + at(kz, e - 1, rows) * at(p0, e - 1, rows)
    pull = pull + (at(kx, e, rows) * at(p0, e, rows, 1) + at(kx, e, rows, -1) * at(p0, e, rows, -1))
    pull = pull + (y * ahead + preceding(y * p, 1))
    put(p_next, e, ahead)
    put(u0, e, p - at(inverse, e, rows) * pull)


def products(e, rows, totals, faces, diag, p0, u0, u_next):
    kx, ky, kz = faces
    p, u = at(p0, e, rows), at(u0, e, rows)
    d = at(diag, e - HALO, rows)
    dp, du = d * p, d * u
    ahead = following(u, 1)
    pull = at(kz, e, rows) * at(u0, e + 1, rows) + at(kx, e, rows) * at(u0, e, rows, 1) + at(ky, e, rows) * ahead
    put(u_next, e, ahead)
    terms = (dp * p, dp * u, du * u, pull * u)
    return tuple(a + t.reshape(-1, 8, t.shape[-1]).sum(0) for a, t in zip(totals, terms))


def split_kernel(rim, early, vp, rims, inner, ahead, rest):
    layers = vp.shape[0]
    rims[:rim] = vp[:rim]
    rims[rim:] = vp[layers - rim :]
    inner[...] = vp[rim : layers - rim]
    ahead[...] = vp[rim : rim + early]
    rest[...] = vp[rim + early : layers - rim]


def border_kernel(tissue, conc, low, high, labels, sems):
    layers, rows, _ = tissue.shape
    copies = []
    for side, out, first, start in ((0, low, 0, 0), (1, high, layers - HALO, layers - TSTEPS)):
        copies.append(pltpu.make_async_copy(tissue.at[pl.ds(first, HALO)], labels.at[side], sems.at[side, 0]))
        for j in range(TSTEPS):
            spot = pl.ds((HALO + j) * rows, rows)
            copies.append(pltpu.make_async_copy(conc.at[start + j], out.at[spot, :], sems.at[side, 1 + j]))
    for copy in copies:
        copy.start()
    for copy in copies:
        copy.wait()
    for side, out in ((0, low), (1, high)):
        for j in range(HALO):
            out[j * rows : (j + 1) * rows, :] = labels[side, j].astype(jnp.float32)


def constants(cond_t, leak_t):
    cond_v = [cond_t[i] for i in range(3)]
    leak_v = [leak_t[i] for i in range(3)]
    diag_v = [6.0 * c * c + k for c, k in zip(cond_v, leak_v)]
    inverse_v = [1.0 / d for d in diag_v]
    ratio_v = [k / d for k, d in zip(leak_v, diag_v)]
    return cond_v, diag_v, inverse_v, ratio_v


def level(e, c, ends, kx, ky):
    put(kx, e, jnp.where(ends[0][1], 0.0, c * following(c, 0)))
    put(ky, e, jnp.where(ends[1][1], 0.0, c * following(c, 1)))


def remaining(rate, diffuse, ends):
    stay = 1.0 - rate
    for low, high in ends:
        stay = stay - jnp.where(low, diffuse, 0.0) - jnp.where(high, diffuse, 0.0)
    return stay


def prepare_kernel(rows, cond_t, leak_t, bind_t, diffuse_t, tissue, conc, kx, ky, kz, diag, inverse, ratio, rate, keep, wide):
    shape = (rows, tissue.shape[1])
    layers = tissue.shape[0] // rows
    cond_v, diag_v, inverse_v, ratio_v = constants(cond_t, leak_t)
    rate_v = [bind_t[0, i] * DT for i in range(3)]
    ends = edges(shape)
    base = remaining(0.0, diffuse_t[0] * DT, ends)

    def own(i, before):
        e = i + HALO
        labels = at(tissue, i, rows)
        c = select(labels, cond_v)
        r = select(labels, rate_v)
        put(diag, i, select(labels, diag_v))
        put(inverse, e, select(labels, inverse_v))
        put(ratio, i, select(labels, ratio_v))
        put(rate, i, r)
        put(keep, i + 1, base - r)
        put(wide, i + TSTEPS, at(conc, i, rows))
        level(e, c, ends, kx, ky)
        put(kz, e - 1, before * c)
        return c

    lax.fori_loop(0, layers, own, jnp.zeros(shape, jnp.float32), unroll=2)


def rim_kernel(parts, rim, width, rows, cond_t, leak_t, bind_t, diffuse_t, blocks, near, far, tissue, diag, ratio, *refs):
    kx, ky, kz, inverse, keep, wide, p0, u0, p_next, u_next, sums, from_low, from_high = refs[6:]
    odd = is_odd()
    from_low[...] = jnp.where(odd, near[...], far[...])
    from_high[...] = jnp.where(odd, far[...], near[...])
    lanes = tissue.shape[1]
    layers = tissue.shape[0] // rows
    me = lax.axis_index("size")
    has_low, has_high = inside()
    cond_v, _, inverse_v, ratio_v = constants(cond_t, leak_t)
    rate_v = [bind_t[0, i] * DT for i in range(3)]
    tis_at = parts * HALO * width
    conc_at = tis_at + HALO * rows
    ends = edges((rows, lanes))

    def labels_of(side, j):
        return side[tis_at + j * rows : tis_at + (j + 1) * rows, :]

    def halo(side, j, e, valid):
        labels = labels_of(side, j)
        c = select(labels, cond_v) * valid
        level(e, c, ends, kx, ky)
        put(inverse, e, select(labels, inverse_v))
        return c

    low = [halo(from_low, j, j, has_low) for j in range(HALO)] + [select(at(tissue, 0, rows), cond_v)]
    high = [select(at(tissue, layers - 1, rows), cond_v)] + [halo(from_high, j, layers + HALO + j, has_high) for j in range(HALO)]
    for j in range(HALO):
        put(kz, j, low[j] * low[j + 1])
        put(kz, layers + HALO - 1 + j, high[j] * high[j + 1])
    for side, j, layer in ((from_low, HALO - 1, 0), (from_high, 0, layers + 1)):
        put(keep, layer, remaining(select(labels_of(side, j), rate_v), diffuse_t[0] * DT, ends))
    for j in range(TSTEPS):
        span = slice(conc_at + j * rows, conc_at + (j + 1) * rows)
        put(wide, j, from_low[span, :])
        put(wide, layers + TSTEPS + j, from_high[span, :])

    for k in range(parts):
        column = pl.multiple_of((me ^ k) * width, width)

        def spot(layer):
            return pl.ds(pl.multiple_of(layer * rows + column, width), width)

        for i in range(rim):
            top = i + (layers - rim)
            p0[spot(i + HALO), :] = blocks[k * 2 * rim + i] * ratio[spot(i), :]
            p0[spot(top + HALO), :] = blocks[k * 2 * rim + rim + i] * ratio[spot(top), :]
        for j in range(HALO):
            span = slice((k * HALO + j) * width, (k * HALO + j + 1) * width)
            for side, e in ((from_low, j), (from_high, layers + HALO + j)):
                labels = side[pl.ds(pl.multiple_of(tis_at + j * rows + column, width), width), :]
                p0[spot(e), :] = side[span, :] * select(labels, ratio_v)

    faces = (kx, ky, kz)

    def both(e, carry):
        image(e, rows, faces, inverse, p0, u0, p_next)
        image(layers + 2 * HALO - 1 - e, rows, faces, inverse, p0, u0, p_next)
        return carry

    lax.fori_loop(1, rim + HALO - 1, both, 0)
    for e in (HALO - 1, layers + HALO):
        put(u_next, e, following(at(u0, e, rows), 1))

    def sum_over(first, count, totals):
        def body(i, carry):
            return products(i + HALO, rows, carry, faces, diag, p0, u0, u_next)

        return lax.fori_loop(first, first + count, body, totals)

    zero = jnp.zeros((8, lanes), jnp.float32)
    totals = sum_over(0, rim - 2, (zero,) * 4)
    totals = sum_over(layers - rim + 1, rim - 1, totals)
    for i in range(4):
        sums[i] = totals[i]


def core_kernel(parts, rim, rows, vp, *refs):
    inner, refs = refs[:parts], refs[parts:]
    kx, ky, kz, diag, inverse, ratio, part = refs[:7]
    p0, u0, p_next, u_next, sums = refs[11:]
    layers, width, _ = vp.shape
    me = lax.axis_index("size")
    sources = [[vp.at[rim : layers - rim]], [inner[0]], [inner[1], inner[2]]] + [[ref] for ref in inner[3:]]
    for k, pieces in enumerate(sources):
        column = pl.multiple_of((me ^ k) * width, width)

        def spot(layer):
            return pl.ds(pl.multiple_of(layer * rows + column, width), width)

        layer = rim
        for piece in pieces:
            for i in range(piece.shape[0]):
                p0[spot(layer + HALO), :] = piece[i] * ratio[spot(layer), :]
                layer += 1

    faces = (kx, ky, kz)
    first = rim + HALO - 1
    last = layers - rim + HALO

    def terms(e, totals):
        return products(e, rows, totals, faces, diag, p0, u0, u_next)

    def picture(e):
        image(e, rows, faces, inverse, p0, u0, p_next)

    def body(i, totals):
        e = first + 2 * i
        totals = terms(e - 2, terms(e - 3, totals))
        picture(e)
        picture(e + 1)
        return totals

    picture(first)
    picture(first + 1)
    pairs = (last + 1 - first) // 2
    totals = lax.fori_loop(1, pairs, body, tuple(part[i] for i in range(4)))
    done = first + 2 * pairs
    for e in range(done, last + 1):
        picture(e)
    for e in range(done - 3, last + 1):
        totals = terms(e, totals)
    sums[...] = jnp.concatenate([t.sum(0, keepdims=True) for t in totals] * 2, 0)


def slide_kernel(rows, wide, low, high):
    def body(i, carry):
        conc = at(wide, i + 1, rows)
        put(low, i, preceding(conc, 1))
        put(high, i, following(conc, 1))
        return carry

    lax.fori_loop(0, low.shape[0] // rows, body, 0, unroll=2)


def transport_kernel(width, rows, hinder_t, diffuse_t, mine, theirs, p0, u0, p_next, u_next, kx, ky, kz, rate, keep, wide, wide_low, wide_high, bound, pressure, free_out, bound_out, press, first, kept, zo, zb, xo, xb, yo, yb):
    lanes = bound.shape[1]
    layers = bound.shape[0] // rows
    me = lax.axis_index("size")
    has_low, has_high = inside()
    sums = mine[...] + theirs[...]
    rho, drop, second, shared = [jnp.sum(sums[i : i + 1, :], axis=1, keepdims=True) for i in range(4)]
    third = second - 2.0 * shared
    alpha = rho / drop
    rho_next = alpha * alpha * second - rho
    beta = rho_next / rho
    curve = drop - 2.0 * alpha * second + alpha * alpha * third - beta * rho_next / alpha
    alpha_next = rho_next / curve
    on_p = jnp.broadcast_to(alpha + alpha_next * (1.0 + beta), (8, lanes))[None]
    on_u = jnp.broadcast_to(-alpha_next * alpha, (8, lanes))[None]
    diffuse = diffuse_t[0] * DT
    hinder = hinder_t[0] * DT

    def combine(p, u, by_p, by_u):
        return (by_p * p.reshape(-1, 8, lanes) + by_u * u.reshape(-1, 8, lanes)).reshape(p.shape)

    def own(i, carry):
        spot = pl.ds(pl.multiple_of((i + HALO) * rows + me * width, width), width)
        put(pressure, i, combine(p0[spot, :], u0[spot, :], on_p, on_u))
        return carry

    lax.fori_loop(0, layers, own, 0, unroll=8)
    drive_p, drive_u = hinder * on_p, hinder * on_u

    def halves(flow, through):
        out = jnp.maximum(flow, 0.0) + through
        return out, out - flow

    def near(ref, layer, shift=0):
        return at(ref, layer, rows, shift)

    def store(ref, layer, value):
        put(ref, layer, value)

    def drive(e):
        store(press, e, combine(near(p0, e), near(u0, e), drive_p, drive_u))

    lane = lax.broadcasted_iota(jnp.int32, (rows, lanes), 1)
    row = lax.broadcasted_iota(jnp.int32, (rows, lanes), 0)
    along = jnp.where(row == rows - 1, 0.0, diffuse)
    rising = jnp.where(lane == lanes - 1, 0.0, diffuse)
    falling = jnp.where(lane == 0, 0.0, diffuse)

    def advance(i):
        e = i + TSTEPS
        here, conc = near(press, e), near(wide, i + 1)
        z_out, z_back = near(zo, i), near(zb, i)
        z_up, z_down = halves(near(kz, e) * (here - near(press, e + 1)), diffuse)
        stay = near(keep, i) - z_up - z_back
        moved = z_out * near(wide, i) + z_down * near(wide, i + 2)
        out, back = halves(near(kx, e) * (here - near(press, e, 1)), along)
        into = preceding(out, 0)
        stay = stay - out - preceding(back, 0)
        moved = moved + into * near(wide, i + 1, -1) + back * near(wide, i + 1, 1)
        flow = near(ky, e) * (here - combine(near(p_next, e), near(u_next, e), drive_p, drive_u))
        out, y_back = halves(flow, rising)
        y_into, y_low = halves(preceding(flow, 1), falling)
        stay = stay - out - y_low
        moved = moved + y_into * near(wide_low, i) + y_back * near(wide_high, i)
        drive(e + 2)
        for ref, value in ((zo, z_up), (zb, z_down), (xo, into), (xb, back), (yo, y_into), (yb, y_back), (kept, stay)):
            store(ref, i + 1, value)
        valid = jnp.where(i == 0, has_low, jnp.where(i == layers + 1, has_high, 1.0))
        store(first, i + 1, (stay * conc + moved) * valid)

    def finish(i):
        here = near(first, i + 1)
        result = near(kept, i + 1) * here + near(zo, i) * near(first, i) + near(zb, i + 1) * near(first, i + 2)
        result = result + near(xo, i + 1) * near(first, i + 1, -1) + near(xb, i + 1) * near(first, i + 1, 1)
        result = result + near(yo, i + 1) * preceding(here, 1) + near(yb, i + 1) * following(here, 1)
        store(free_out, i - 1, result)
        gain = near(rate, i - 1) * (near(wide, i + 1) + here)
        store(bound_out, i - 1, near(bound, i - 1) + gain)

    for e in range(TSTEPS - 1, TSTEPS + 2):
        drive(e)
    z_out, z_back = halves(near(kz, TSTEPS - 1) * (near(press, TSTEPS - 1) - near(press, TSTEPS)), diffuse)
    store(zo, 0, z_out)
    store(zb, 0, z_back)

    def begin(i, carry):
        advance(i)
        return carry

    lax.fori_loop(0, 3, begin, 0)

    def body(i, carry):
        finish(i - 2)
        advance(i)
        return carry

    lax.fori_loop(3, layers + 2, body, 0)
    finish(layers)


def swapped(array, axis, bit):
    count = lax.axis_size(axis)
    return lax.ppermute(array, axis, [(i, i ^ bit) for i in range(count)])


def butterfly(array, axis):
    bit = 1
    while bit < lax.axis_size(axis):
        array = jnp.concatenate([array, swapped(array, axis, bit)], 0)
        bit *= 2
    return array


def is_odd():
    return lax.rem(lax.axis_index("gz"), 2) == 1


def across(low, high):
    count = lax.axis_size("gz")
    pairs = [(i, i ^ 1) for i in range(count)]
    near = lax.ppermute(jnp.where(is_odd(), low, high), "gz", pairs)
    pairs = [(i, i + 1) for i in range(1, count - 1, 2)]
    far = lax.ppermute(jnp.where(is_odd(), high, low), "gz", pairs + [(j, i) for i, j in pairs])
    return near, far


def total_over(array, axis):
    count = lax.axis_size(axis)
    step = 1
    while True:
        other = swapped(array, axis, step)
        step *= 2
        if step == count:
            return array, other
        array = array + other


def smem():
    return pl.BlockSpec(memory_space=pltpu.SMEM)


def vmem():
    return pl.BlockSpec(memory_space=pltpu.VMEM)


def f32(*shape):
    return jax.ShapeDtypeStruct(shape, jnp.float32)


def call(kernel, outs, scalars, arrays, scratch=(), aliases={}):
    size = sum(4 * math.prod(a.shape) for a in list(outs) + list(arrays) + list(scratch))
    return pl.pallas_call(
        kernel,
        out_shape=tuple(outs),
        in_specs=[smem()] * len(scalars) + [vmem()] * len(arrays),
        out_specs=(vmem(),) * len(outs),
        scratch_shapes=[pltpu.VMEM(s.shape, s.dtype) for s in scratch],
        input_output_aliases=aliases,
        compiler_params=pltpu.CompilerParams(vmem_limit_bytes=size + (4 << 20)),
    )(*scalars, *arrays)


def program(tissue, vessel_pressure, cond_table, leak_table, bind_table, hindrance, diffusivity, free_conc, bound_conc):
    layers, width, lanes = vessel_pressure.shape
    rows = tissue.shape[1]
    parts = rows // width
    rim = HALO
    conc, bound = free_conc[0], bound_conc[0]
    slab = f32(layers * rows, lanes)
    extended = f32((layers + 2 * HALO) * rows, lanes)
    stepped = f32((layers + 2) * rows, lanes)
    wider = f32((layers + 2 * TSTEPS) * rows, lanes)
    count = layers - 2 * rim
    early = EARLY * count // 32
    rims, middle, ahead, rest = call(
        functools.partial(split_kernel, rim, early),
        [f32(2 * rim, width, lanes), f32(count, width, lanes), f32(early, width, lanes), f32(count - early, width, lanes)],
        [],
        [vessel_pressure],
    )
    blocks = butterfly(rims, "size")
    inner = [(swapped(middle, "size", k),) for k in range(1, parts)]
    inner[1] = (swapped(ahead, "size", 2), swapped(rest, "size", 2))
    inner = [piece for pieces in inner for piece in pieces]
    border = f32((HALO + TSTEPS) * rows, lanes)
    border_low, border_high = pl.pallas_call(
        border_kernel,
        out_shape=(border,) * 2,
        in_specs=[pl.BlockSpec(memory_space=pltpu.HBM)] * 2,
        out_specs=(vmem(),) * 2,
        scratch_shapes=[pltpu.VMEM((2, HALO, rows, lanes), jnp.int32), pltpu.SemaphoreType.DMA((2, 1 + TSTEPS))],
        compiler_params=pltpu.CompilerParams(vmem_limit_bytes=8 << 20),
        name="border",
    )(pltpu.with_memory_space_constraint(tissue, pltpu.HBM), pltpu.with_memory_space_constraint(conc, pltpu.HBM))

    def payload(first, border):
        pieces = [blocks[k * 2 * rim + first : k * 2 * rim + first + HALO] for k in range(parts)] + [border]
        return jnp.concatenate([a.reshape(-1, lanes) for a in pieces], 0)

    near, far = across(payload(0, border_low), payload(2 * rim - HALO, border_high))
    tissue, conc, bound = (a.reshape(-1, lanes) for a in (tissue, conc, bound))
    kx, ky, kz, diag, inverse, ratio, rate, keep, wide = call(
        functools.partial(prepare_kernel, rows),
        [extended] * 3 + [slab, extended, slab, slab, stepped, wider],
        [cond_table, leak_table, bind_table, diffusivity],
        [tissue, conc],
    )
    kx, ky, kz, inverse, keep, wide, p0, u0, p_next, u_next, part = call(
        functools.partial(rim_kernel, parts, rim, width, rows),
        [extended] * 4 + [stepped, wider] + [extended] * 4 + [f32(4, 8, lanes)],
        [cond_table, leak_table, bind_table, diffusivity],
        [blocks, near, far, tissue, diag, ratio, kx, ky, kz, inverse, keep, wide],
        scratch=[f32(*near.shape)] * 2,
        aliases={10 + i: i for i in range(6)},
    )
    p0, u0, p_next, u_next, sums = call(
        functools.partial(core_kernel, parts, rim, rows),
        [extended] * 4 + [f32(8, lanes)],
        [],
        [vessel_pressure, *inner, kx, ky, kz, diag, inverse, ratio, part, p0, u0, p_next, u_next],
        aliases={parts + 8 + i: i for i in range(4)},
    )
    wide_low, wide_high = call(functools.partial(slide_kernel, rows), [stepped] * 2, [], [wide])
    mine, theirs = total_over(sums, "gz")
    pressure, free, bound = call(
        functools.partial(transport_kernel, width, rows),
        [f32(layers * width, lanes), slab, slab],
        [hindrance, diffusivity],
        [mine, theirs, p0, u0, p_next, u_next, kx, ky, kz, rate, keep, wide, wide_low, wide_high, bound],
        scratch=[f32((layers + 2 * HALO + 1) * rows, lanes)] + [wider] * 8,
    )
    shape = (1, layers, rows, lanes)
    return pressure.reshape(layers, width, lanes), free.reshape(shape), bound.reshape(shape)


def solution(mesh):
    return jax.shard_map(
        program,
        mesh=mesh,
        in_specs=(
            P("gz", None, None),
            P("gz", "size", None),
            P(),
            P(),
            P("size", None),
            P("size"),
            P("size"),
            P("size", "gz", None, None),
            P("size", "gz", None, None),
        ),
        out_specs=(P("gz", "size", None), P("size", "gz", None, None), P("size", "gz", None, None)),
        check_vma=False,
    )
```

```python
import functools
import math
import jax
import jax.numpy as jnp
from jax import lax
from jax.experimental import pallas as pl
from jax.experimental.pallas import tpu as pltpu
from jax.sharding import PartitionSpec as P

TSTEPS = 2
HALO = TSTEPS + 1
DT = 0.1
EARLY = 8


def select(labels, values):
    return jnp.where(labels == 0, values[0], jnp.where(labels == 1, values[1], values[2]))


def following(cells, axis):
    return pltpu.roll(cells, cells.shape[axis] - 1, axis)


def preceding(cells, axis):
    return pltpu.roll(cells, 1, axis)


def edges(shape):
    row = lax.broadcasted_iota(jnp.int32, shape, 0)
    lane = lax.broadcasted_iota(jnp.int32, shape, 1)
    return (row == 0, row == shape[0] - 1), (lane == 0, lane == shape[1] - 1)


def inside():
    slab = lax.axis_index("gz")
    has_low = (slab > 0).astype(jnp.float32)
    has_high = (slab < lax.axis_size("gz") - 1).astype(jnp.float32)
    return has_low, has_high


def at(ref, layer, rows, shift=0):
    if shift == 0:
        return ref[pl.ds(pl.multiple_of(layer * rows, 8), rows), :]
    view = ref.at[pl.ds(pl.multiple_of(layer * rows - 8, 8), rows + 16), :]
    return view[8 + shift : 8 + shift + rows, :]


def put(ref, layer, value):
    rows = value.shape[0]
    ref[pl.ds(pl.multiple_of(layer * rows, 8), rows), :] = value


def image(e, rows, faces, inverse, p0, u0, p_next):
    kx, ky, kz = faces
    p, y = at(p0, e, rows), at(ky, e, rows)
    ahead = following(p, 1)
    pull = at(kz, e, rows) * at(p0, e + 1, rows) + at(kz, e - 1, rows) * at(p0, e - 1, rows)
    pull = pull + (at(kx, e, rows) * at(p0, e, rows, 1) + at(kx, e, rows, -1) * at(p0, e, rows, -1))
    pull = pull + (y * ahead + preceding(y * p, 1))
    put(p_next, e, ahead)
    put(u0, e, p - at(inverse, e, rows) * pull)


def products(e, rows, totals, faces, diag, p0, u0, u_next):
    kx, ky, kz = faces
    p, u = at(p0, e, rows), at(u0, e, rows)
    d = at(diag, e - HALO, rows)
    dp, du = d * p, d * u
    ahead = following(u, 1)
    pull = at(kz, e, rows) * at(u0, e + 1, rows) + at(kx, e, rows) * at(u0, e, rows, 1) + at(ky, e, rows) * ahead
    put(u_next, e, ahead)
    terms = (dp * p, dp * u, du * u, pull * u)
    return tuple(a + t.reshape(-1, 8, t.shape[-1]).sum(0) for a, t in zip(totals, terms))


def split_kernel(rim, early, vp, rims, inner, ahead, rest):
    layers = vp.shape[0]
    rims[:rim] = vp[:rim]
    rims[rim:] = vp[layers - rim :]
    inner[...] = vp[rim : layers - rim]
    ahead[...] = vp[rim : rim + early]
    rest[...] = vp[rim + early : layers - rim]


def border_kernel(tissue, conc, low, high, labels, sems):
    layers, rows, _ = tissue.shape
    copies = []
    for side, out, first, start in ((0, low, 0, 0), (1, high, layers - HALO, layers - TSTEPS)):
        copies.append(pltpu.make_async_copy(tissue.at[pl.ds(first, HALO)], labels.at[side], sems.at[side, 0]))
        for j in range(TSTEPS):
            spot = pl.ds((HALO + j) * rows, rows)
            copies.append(pltpu.make_async_copy(conc.at[start + j], out.at[spot, :], sems.at[side, 1 + j]))
    for copy in copies:
        copy.start()
    for copy in copies:
        copy.wait()
    for side, out in ((0, low), (1, high)):
        for j in range(HALO):
            out[j * rows : (j + 1) * rows, :] = labels[side, j].astype(jnp.float32)


def constants(cond_t, leak_t):
    cond_v = [cond_t[i] for i in range(3)]
    leak_v = [leak_t[i] for i in range(3)]
    diag_v = [6.0 * c * c + k for c, k in zip(cond_v, leak_v)]
    inverse_v = [1.0 / d for d in diag_v]
    ratio_v = [k / d for k, d in zip(leak_v, diag_v)]
    return cond_v, diag_v, inverse_v, ratio_v


def level(e, c, ends, kx, ky):
    put(kx, e, jnp.where(ends[0][1], 0.0, c * following(c, 0)))
    put(ky, e, jnp.where(ends[1][1], 0.0, c * following(c, 1)))


def remaining(rate, diffuse, ends):
    stay = 1.0 - rate
    for low, high in ends:
        stay = stay - jnp.where(low, diffuse, 0.0) - jnp.where(high, diffuse, 0.0)
    return stay


def prepare_kernel(rows, cond_t, leak_t, bind_t, diffuse_t, tissue, conc, kx, ky, kz, diag, inverse, ratio, rate, keep, wide):
    shape = (rows, tissue.shape[1])
    layers = tissue.shape[0] // rows
    cond_v, diag_v, inverse_v, ratio_v = constants(cond_t, leak_t)
    rate_v = [bind_t[0, i] * DT for i in range(3)]
    ends = edges(shape)
    base = remaining(0.0, diffuse_t[0] * DT, ends)

    def own(i, before):
        e = i + HALO
        labels = at(tissue, i, rows)
        c = select(labels, cond_v)
        r = select(labels, rate_v)
        put(diag, i, select(labels, diag_v))
        put(inverse, e, select(labels, inverse_v))
        put(ratio, i, select(labels, ratio_v))
        put(rate, i, r)
        put(keep, i + 1, base - r)
        put(wide, i + TSTEPS, at(conc, i, rows))
        level(e, c, ends, kx, ky)
        put(kz, e - 1, before * c)
        return c

    lax.fori_loop(0, layers, own, jnp.zeros(shape, jnp.float32), unroll=2)


def rim_kernel(parts, rim, width, rows, cond_t, leak_t, bind_t, diffuse_t, blocks, near, far, tissue, diag, ratio, *refs):
    kx, ky, kz, inverse, keep, wide, p0, u0, p_next, u_next, sums, from_low, from_high = refs[6:]
    odd = is_odd()
    from_low[...] = jnp.where(odd, near[...], far[...])
    from_high[...] = jnp.where(odd, far[...], near[...])
    lanes = tissue.shape[1]
    layers = tissue.shape[0] // rows
    me = lax.axis_index("size")
    has_low, has_high = inside()
    cond_v, _, inverse_v, ratio_v = constants(cond_t, leak_t)
    rate_v = [bind_t[0, i] * DT for i in range(3)]
    tis_at = parts * HALO * width
    conc_at = tis_at + HALO * rows
    ends = edges((rows, lanes))

    def labels_of(side, j):
        return side[tis_at + j * rows : tis_at + (j + 1) * rows, :]

    def halo(side, j, e, valid):
        labels = labels_of(side, j)
        c = select(labels, cond_v) * valid
        level(e, c, ends, kx, ky)
        put(inverse, e, select(labels, inverse_v))
        return c

    low = [halo(from_low, j, j, has_low) for j in range(HALO)] + [select(at(tissue, 0, rows), cond_v)]
    high = [select(at(tissue, layers - 1, rows), cond_v)] + [halo(from_high, j, layers + HALO + j, has_high) for j in range(HALO)]
    for j in range(HALO):
        put(kz, j, low[j] * low[j + 1])
        put(kz, layers + HALO - 1 + j, high[j] * high[j + 1])
    for side, j, layer in ((from_low, HALO - 1, 0), (from_high, 0, layers + 1)):
        put(keep, layer, remaining(select(labels_of(side, j), rate_v), diffuse_t[0] * DT, ends))
    for j in range(TSTEPS):
        span = slice(conc_at + j * rows, conc_at + (j + 1) * rows)
        put(wide, j, from_low[span, :])
        put(wide, layers + TSTEPS + j, from_high[span, :])

    for k in range(parts):
        column = pl.multiple_of((me ^ k) * width, width)

        def spot(layer):
            return pl.ds(pl.multiple_of(layer * rows + column, width), width)

        for i in range(rim):
            top = i + (layers - rim)
            p0[spot(i + HALO), :] = blocks[k * 2 * rim + i] * ratio[spot(i), :]
            p0[spot(top + HALO), :] = blocks[k * 2 * rim + rim + i] * ratio[spot(top), :]
        for j in range(HALO):
            span = slice((k * HALO + j) * width, (k * HALO + j + 1) * width)
            for side, e in ((from_low, j), (from_high, layers + HALO + j)):
                labels = side[pl.ds(pl.multiple_of(tis_at + j * rows + column, width), width), :]
                p0[spot(e), :] = side[span, :] * select(labels, ratio_v)

    faces = (kx, ky, kz)

    def both(e, carry):
        image(e, rows, faces, inverse, p0, u0, p_next)
        image(layers + 2 * HALO - 1 - e, rows, faces, inverse, p0, u0, p_next)
        return carry

    lax.fori_loop(1, rim + HALO - 1, both, 0)
    for e in (HALO - 1, layers + HALO):
        put(u_next, e, following(at(u0, e, rows), 1))

    def sum_over(first, count, totals):
        def body(i, carry):
            return products(i + HALO, rows, carry, faces, diag, p0, u0, u_next)

        return lax.fori_loop(first, first + count, body, totals)

    zero = jnp.zeros((8, lanes), jnp.float32)
    totals = sum_over(0, rim - 2, (zero,) * 4)
    totals = sum_over(layers - rim + 1, rim - 1, totals)
    for i in range(4):
        sums[i] = totals[i]


def core_kernel(parts, rim, rows, vp, *refs):
    inner, refs = refs[:parts], refs[parts:]
    kx, ky, kz, diag, inverse, ratio, part = refs[:7]
    p0, u0, p_next, u_next, sums = refs[11:]
    layers, width, _ = vp.shape
    me = lax.axis_index("size")
    sources = [[vp.at[rim : layers - rim]], [inner[0]], [inner[1], inner[2]]] + [[ref] for ref in inner[3:]]
    for k, pieces in enumerate(sources):
        column = pl.multiple_of((me ^ k) * width, width)

        def spot(layer):
            return pl.ds(pl.multiple_of(layer * rows + column, width), width)

        layer = rim
        for piece in pieces:
            for i in range(piece.shape[0]):
                p0[spot(layer + HALO), :] = piece[i] * ratio[spot(layer), :]
                layer += 1

    faces = (kx, ky, kz)
    first = rim + HALO - 1
    last = layers - rim + HALO

    def terms(e, totals):
        return products(e, rows, totals, faces, diag, p0, u0, u_next)

    def picture(e):
        image(e, rows, faces, inverse, p0, u0, p_next)

    def body(i, totals):
        e = first + 2 * i
        totals = terms(e - 2, terms(e - 3, totals))
        picture(e)
        picture(e + 1)
        return totals

    picture(first)
    picture(first + 1)
    pairs = (last + 1 - first) // 2
    totals = lax.fori_loop(1, pairs, body, tuple(part[i] for i in range(4)))
    done = first + 2 * pairs
    for e in range(done, last + 1):
        picture(e)
    for e in range(done - 3, last + 1):
        totals = terms(e, totals)
    sums[...] = jnp.concatenate([t.sum(0, keepdims=True) for t in totals] * 2, 0)


def slide_kernel(rows, wide, low, high):
    def body(i, carry):
        conc = at(wide, i + 1, rows)
        put(low, i, preceding(conc, 1))
        put(high, i, following(conc, 1))
        return carry

    lax.fori_loop(0, low.shape[0] // rows, body, 0, unroll=2)


def transport_kernel(width, rows, hinder_t, diffuse_t, mine, theirs, p0, u0, p_next, u_next, kx, ky, kz, rate, keep, wide, wide_low, wide_high, bound, pressure, free_out, bound_out, press, first, kept, zo, zb, xo, xb, yo, yb):
    lanes = bound.shape[1]
    layers = bound.shape[0] // rows
    me = lax.axis_index("size")
    has_low, has_high = inside()
    sums = mine[...] + theirs[...]
    rho, drop, second, shared = [jnp.sum(sums[i : i + 1, :], axis=1, keepdims=True) for i in range(4)]
    third = second - 2.0 * shared
    alpha = rho / drop
    rho_next = alpha * alpha * second - rho
    beta = rho_next / rho
    curve = drop - 2.0 * alpha * second + alpha * alpha * third - beta * rho_next / alpha
    alpha_next = rho_next / curve
    on_p = jnp.broadcast_to(alpha + alpha_next * (1.0 + beta), (8, lanes))[None]
    on_u = jnp.broadcast_to(-alpha_next * alpha, (8, lanes))[None]
    diffuse = diffuse_t[0] * DT
    hinder = hinder_t[0] * DT

    def combine(p, u, by_p, by_u):
        return (by_p * p.reshape(-1, 8, lanes) + by_u * u.reshape(-1, 8, lanes)).reshape(p.shape)

    def own(i, carry):
        spot = pl.ds(pl.multiple_of((i + HALO) * rows + me * width, width), width)
        put(pressure, i, combine(p0[spot, :], u0[spot, :], on_p, on_u))
        return carry

    lax.fori_loop(0, layers, own, 0, unroll=8)
    drive_p, drive_u = hinder * on_p, hinder * on_u

    def halves(flow, through):
        out = jnp.maximum(flow, 0.0) + through
        return out, out - flow

    def near(ref, layer, shift=0):
        return at(ref, layer, rows, shift)

    def store(ref, layer, value):
        put(ref, layer, value)

    def drive(e):
        store(press, e, combine(near(p0, e), near(u0, e), drive_p, drive_u))

    lane = lax.broadcasted_iota(jnp.int32, (rows, lanes), 1)
    row = lax.broadcasted_iota(jnp.int32, (rows, lanes), 0)
    along = jnp.where(row == rows - 1, 0.0, diffuse)
    rising = jnp.where(lane == lanes - 1, 0.0, diffuse)
    falling = jnp.where(lane == 0, 0.0, diffuse)

    def advance(i, z_out, z_back):
        e = i + TSTEPS
        here, conc = near(press, e), near(wide, i + 1)
        z_up, z_down = halves(near(kz, e) * (here - near(press, e + 1)), diffuse)
        stay = near(keep, i) - z_up - z_back
        moved = z_out * near(wide, i) + z_down * near(wide, i + 2)
        out, back = halves(near(kx, e) * (here - near(press, e, 1)), along)
        into = preceding(out, 0)
        stay = stay - out - preceding(back, 0)
        moved = moved + into * near(wide, i + 1, -1) + back * near(wide, i + 1, 1)
        flow = near(ky, e) * (here - combine(near(p_next, e), near(u_next, e), drive_p, drive_u))
        out, y_back = halves(flow, rising)
        y_into, y_low = halves(preceding(flow, 1), falling)
        stay = stay - out - y_low
        moved = moved + y_into * near(wide_low, i) + y_back * near(wide_high, i)
        for ref, value in ((zo, z_up), (zb, z_down), (xo, into), (xb, back), (yo, y_into), (yb, y_back), (kept, stay)):
            store(ref, i + 1, value)
        valid = jnp.where(i == 0, has_low, jnp.where(i == layers + 1, has_high, 1.0))
        store(first, i + 1, (stay * conc + moved) * valid)
        return z_up, z_down

    def finish(i):
        here = near(first, i + 1)
        result = near(kept, i + 1) * here + near(zo, i) * near(first, i) + near(zb, i + 1) * near(first, i + 2)
        result = result + near(xo, i + 1) * near(first, i + 1, -1) + near(xb, i + 1) * near(first, i + 1, 1)
        result = result + near(yo, i + 1) * preceding(here, 1) + near(yb, i + 1) * following(here, 1)
        store(free_out, i - 1, result)
        gain = near(rate, i - 1) * (near(wide, i + 1) + here)
        store(bound_out, i - 1, near(bound, i - 1) + gain)

    for e in range(TSTEPS - 1, TSTEPS + 3):
        drive(e)
    z_out, z_back = halves(near(kz, TSTEPS - 1) * (near(press, TSTEPS - 1) - near(press, TSTEPS)), diffuse)
    store(zo, 0, z_out)
    store(zb, 0, z_back)

    def two(i):
        z_out, z_back = advance(i, near(zo, i), near(zb, i))
        advance(i + 1, z_out, z_back)
        for step in range(TSTEPS + 3, TSTEPS + 5):
            drive(jnp.minimum(i + step, layers + 2 * TSTEPS))

    def begin(j, carry):
        two(2 * j)
        return carry

    lax.fori_loop(0, 2, begin, 0)

    def body(j, carry):
        finish(2 * j - 3)
        finish(2 * j - 2)
        two(2 * j)
        return carry

    pairs = (layers + 2) // 2
    lax.fori_loop(2, pairs, body, 0)
    for i in range(2 * pairs, layers + 2):
        advance(i, near(zo, i), near(zb, i))
    for i in range(2 * pairs - 3, layers + 1):
        finish(i)


def swapped(array, axis, bit):
    count = lax.axis_size(axis)
    return lax.ppermute(array, axis, [(i, i ^ bit) for i in range(count)])


def butterfly(array, axis):
    bit = 1
    while bit < lax.axis_size(axis):
        array = jnp.concatenate([array, swapped(array, axis, bit)], 0)
        bit *= 2
    return array


def is_odd():
    return lax.rem(lax.axis_index("gz"), 2) == 1


def across(low, high):
    count = lax.axis_size("gz")
    pairs = [(i, i ^ 1) for i in range(count)]
    near = lax.ppermute(jnp.where(is_odd(), low, high), "gz", pairs)
    pairs = [(i, i + 1) for i in range(1, count - 1, 2)]
    far = lax.ppermute(jnp.where(is_odd(), high, low), "gz", pairs + [(j, i) for i, j in pairs])
    return near, far


def total_over(array, axis):
    count = lax.axis_size(axis)
    step = 1
    while True:
        other = swapped(array, axis, step)
        step *= 2
        if step == count:
            return array, other
        array = array + other


def smem():
    return pl.BlockSpec(memory_space=pltpu.SMEM)


def vmem():
    return pl.BlockSpec(memory_space=pltpu.VMEM)


def f32(*shape):
    return jax.ShapeDtypeStruct(shape, jnp.float32)


def call(kernel, outs, scalars, arrays, scratch=(), aliases={}):
    size = sum(4 * math.prod(a.shape) for a in list(outs) + list(arrays) + list(scratch))
    return pl.pallas_call(
        kernel,
        out_shape=tuple(outs),
        in_specs=[smem()] * len(scalars) + [vmem()] * len(arrays),
        out_specs=(vmem(),) * len(outs),
        scratch_shapes=[pltpu.VMEM(s.shape, s.dtype) for s in scratch],
        input_output_aliases=aliases,
        compiler_params=pltpu.CompilerParams(vmem_limit_bytes=size + (4 << 20)),
    )(*scalars, *arrays)


def program(tissue, vessel_pressure, cond_table, leak_table, bind_table, hindrance, diffusivity, free_conc, bound_conc):
    layers, width, lanes = vessel_pressure.shape
    rows = tissue.shape[1]
    parts = rows // width
    rim = HALO
    conc, bound = free_conc[0], bound_conc[0]
    slab = f32(layers * rows, lanes)
    extended = f32((layers + 2 * HALO) * rows, lanes)
    stepped = f32((layers + 2) * rows, lanes)
    wider = f32((layers + 2 * TSTEPS) * rows, lanes)
    count = layers - 2 * rim
    early = EARLY * count // 32
    rims, middle, ahead, rest = call(
        functools.partial(split_kernel, rim, early),
        [f32(2 * rim, width, lanes), f32(count, width, lanes), f32(early, width, lanes), f32(count - early, width, lanes)],
        [],
        [vessel_pressure],
    )
    blocks = butterfly(rims, "size")
    inner = [(swapped(middle, "size", k),) for k in range(1, parts)]
    inner[1] = (swapped(ahead, "size", 2), swapped(rest, "size", 2))
    inner = [piece for pieces in inner for piece in pieces]
    border = f32((HALO + TSTEPS) * rows, lanes)
    border_low, border_high = pl.pallas_call(
        border_kernel,
        out_shape=(border,) * 2,
        in_specs=[pl.BlockSpec(memory_space=pltpu.HBM)] * 2,
        out_specs=(vmem(),) * 2,
        scratch_shapes=[pltpu.VMEM((2, HALO, rows, lanes), jnp.int32), pltpu.SemaphoreType.DMA((2, 1 + TSTEPS))],
        compiler_params=pltpu.CompilerParams(vmem_limit_bytes=8 << 20),
        name="border",
    )(pltpu.with_memory_space_constraint(tissue, pltpu.HBM), pltpu.with_memory_space_constraint(conc, pltpu.HBM))

    def payload(first, border):
        pieces = [blocks[k * 2 * rim + first : k * 2 * rim + first + HALO] for k in range(parts)] + [border]
        return jnp.concatenate([a.reshape(-1, lanes) for a in pieces], 0)

    near, far = across(payload(0, border_low), payload(2 * rim - HALO, border_high))
    tissue, conc, bound = (a.reshape(-1, lanes) for a in (tissue, conc, bound))
    kx, ky, kz, diag, inverse, ratio, rate, keep, wide = call(
        functools.partial(prepare_kernel, rows),
        [extended] * 3 + [slab, extended, slab, slab, stepped, wider],
        [cond_table, leak_table, bind_table, diffusivity],
        [tissue, conc],
    )
    kx, ky, kz, inverse, keep, wide, p0, u0, p_next, u_next, part = call(
        functools.partial(rim_kernel, parts, rim, width, rows),
        [extended] * 4 + [stepped, wider] + [extended] * 4 + [f32(4, 8, lanes)],
        [cond_table, leak_table, bind_table, diffusivity],
        [blocks, near, far, tissue, diag, ratio, kx, ky, kz, inverse, keep, wide],
        scratch=[f32(*near.shape)] * 2,
        aliases={10 + i: i for i in range(6)},
    )
    p0, u0, p_next, u_next, sums = call(
        functools.partial(core_kernel, parts, rim, rows),
        [extended] * 4 + [f32(8, lanes)],
        [],
        [vessel_pressure, *inner, kx, ky, kz, diag, inverse, ratio, part, p0, u0, p_next, u_next],
        aliases={parts + 8 + i: i for i in range(4)},
    )
    wide_low, wide_high = call(functools.partial(slide_kernel, rows), [stepped] * 2, [], [wide])
    mine, theirs = total_over(sums, "gz")
    pressure, free, bound = call(
        functools.partial(transport_kernel, width, rows),
        [f32(layers * width, lanes), slab, slab],
        [hindrance, diffusivity],
        [mine, theirs, p0, u0, p_next, u_next, kx, ky, kz, rate, keep, wide, wide_low, wide_high, bound],
        scratch=[f32((layers + 2 * HALO + 1) * rows, lanes)] + [wider] * 8,
    )
    shape = (1, layers, rows, lanes)
    return pressure.reshape(layers, width, lanes), free.reshape(shape), bound.reshape(shape)


def solution(mesh):
    return jax.shard_map(
        program,
        mesh=mesh,
        in_specs=(
            P("gz", None, None),
            P("gz", "size", None),
            P(),
            P(),
            P("size", None),
            P("size"),
            P("size"),
            P("size", "gz", None, None),
            P("size", "gz", None, None),
        ),
        out_specs=(P("gz", "size", None), P("size", "gz", None, None), P("size", "gz", None, None)),
        check_vma=False,
    )
```

```python
import functools
import math
import jax
import jax.numpy as jnp
from jax import lax
from jax.experimental import pallas as pl
from jax.experimental.pallas import tpu as pltpu
from jax.sharding import PartitionSpec as P

TSTEPS = 2
HALO = TSTEPS + 1
DT = 0.1
EARLY = 10


def select(labels, values):
    return jnp.where(labels == 0, values[0], jnp.where(labels == 1, values[1], values[2]))


def following(cells, axis):
    return pltpu.roll(cells, cells.shape[axis] - 1, axis)


def preceding(cells, axis):
    return pltpu.roll(cells, 1, axis)


def edges(shape):
    row = lax.broadcasted_iota(jnp.int32, shape, 0)
    lane = lax.broadcasted_iota(jnp.int32, shape, 1)
    return (row == 0, row == shape[0] - 1), (lane == 0, lane == shape[1] - 1)


def inside():
    slab = lax.axis_index("gz")
    has_low = (slab > 0).astype(jnp.float32)
    has_high = (slab < lax.axis_size("gz") - 1).astype(jnp.float32)
    return has_low, has_high


def at(ref, layer, rows, shift=0):
    if shift == 0:
        return ref[pl.ds(pl.multiple_of(layer * rows, 8), rows), :]
    view = ref.at[pl.ds(pl.multiple_of(layer * rows - 8, 8), rows + 16), :]
    return view[8 + shift : 8 + shift + rows, :]


def put(ref, layer, value):
    rows = value.shape[0]
    ref[pl.ds(pl.multiple_of(layer * rows, 8), rows), :] = value


def image(e, rows, faces, inverse, p0, u0, p_next):
    kx, ky, kz = faces
    p, y = at(p0, e, rows), at(ky, e, rows)
    ahead = following(p, 1)
    pull = at(kz, e, rows) * at(p0, e + 1, rows) + at(kz, e - 1, rows) * at(p0, e - 1, rows)
    pull = pull + (at(kx, e, rows) * at(p0, e, rows, 1) + at(kx, e, rows, -1) * at(p0, e, rows, -1))
    pull = pull + (y * ahead + preceding(y * p, 1))
    put(p_next, e, ahead)
    put(u0, e, p - at(inverse, e, rows) * pull)


def products(e, rows, totals, faces, diag, p0, u0, u_next):
    kx, ky, kz = faces
    p, u = at(p0, e, rows), at(u0, e, rows)
    d = at(diag, e - HALO, rows)
    dp, du = d * p, d * u
    ahead = following(u, 1)
    pull = at(kz, e, rows) * at(u0, e + 1, rows) + at(kx, e, rows) * at(u0, e, rows, 1) + at(ky, e, rows) * ahead
    put(u_next, e, ahead)
    terms = (dp * p, dp * u, du * u, pull * u)
    return tuple(a + t.reshape(-1, 8, t.shape[-1]).sum(0) for a, t in zip(totals, terms))


def split_kernel(rim, early, vp, rims, inner, ahead, rest):
    layers = vp.shape[0]
    rims[:rim] = vp[:rim]
    rims[rim:] = vp[layers - rim :]
    inner[...] = vp[rim : layers - rim]
    ahead[...] = vp[rim : rim + early]
    rest[...] = vp[rim + early : layers - rim]


def border_kernel(tissue, conc, low, high, labels, sems):
    layers, rows, _ = tissue.shape
    copies = []
    for side, out, first, start in ((0, low, 0, 0), (1, high, layers - HALO, layers - TSTEPS)):
        copies.append(pltpu.make_async_copy(tissue.at[pl.ds(first, HALO)], labels.at[side], sems.at[side, 0]))
        for j in range(TSTEPS):
            spot = pl.ds((HALO + j) * rows, rows)
            copies.append(pltpu.make_async_copy(conc.at[start + j], out.at[spot, :], sems.at[side, 1 + j]))
    for copy in copies:
        copy.start()
    for copy in copies:
        copy.wait()
    for side, out in ((0, low), (1, high)):
        for j in range(HALO):
            out[j * rows : (j + 1) * rows, :] = labels[side, j].astype(jnp.float32)


def constants(cond_t, leak_t):
    cond_v = [cond_t[i] for i in range(3)]
    leak_v = [leak_t[i] for i in range(3)]
    diag_v = [6.0 * c * c + k for c, k in zip(cond_v, leak_v)]
    inverse_v = [1.0 / d for d in diag_v]
    ratio_v = [k / d for k, d in zip(leak_v, diag_v)]
    return cond_v, diag_v, inverse_v, ratio_v


def level(e, c, ends, kx, ky):
    put(kx, e, jnp.where(ends[0][1], 0.0, c * following(c, 0)))
    put(ky, e, jnp.where(ends[1][1], 0.0, c * following(c, 1)))


def remaining(rate, diffuse, ends):
    stay = 1.0 - rate
    for low, high in ends:
        stay = stay - jnp.where(low, diffuse, 0.0) - jnp.where(high, diffuse, 0.0)
    return stay


def prepare_kernel(rows, cond_t, leak_t, bind_t, diffuse_t, tissue, conc, kx, ky, kz, diag, inverse, ratio, rate, keep, wide):
    shape = (rows, tissue.shape[1])
    layers = tissue.shape[0] // rows
    cond_v, diag_v, inverse_v, ratio_v = constants(cond_t, leak_t)
    rate_v = [bind_t[0, i] * DT for i in range(3)]
    ends = edges(shape)
    base = remaining(0.0, diffuse_t[0] * DT, ends)

    def own(i, before):
        e = i + HALO
        labels = at(tissue, i, rows)
        c = select(labels, cond_v)
        r = select(labels, rate_v)
        put(diag, i, select(labels, diag_v))
        put(inverse, e, select(labels, inverse_v))
        put(ratio, i, select(labels, ratio_v))
        put(rate, i, r)
        put(keep, i + 1, base - r)
        put(wide, i + TSTEPS, at(conc, i, rows))
        level(e, c, ends, kx, ky)
        put(kz, e - 1, before * c)
        return c

    lax.fori_loop(0, layers, own, jnp.zeros(shape, jnp.float32), unroll=4)


def rim_kernel(parts, rim, width, rows, cond_t, leak_t, bind_t, diffuse_t, blocks, near, far, tissue, diag, ratio, *refs):
    kx, ky, kz, inverse, keep, wide, p0, u0, p_next, u_next, sums, from_low, from_high = refs[6:]
    odd = is_odd()
    from_low[...] = jnp.where(odd, near[...], far[...])
    from_high[...] = jnp.where(odd, far[...], near[...])
    lanes = tissue.shape[1]
    layers = tissue.shape[0] // rows
    me = lax.axis_index("size")
    has_low, has_high = inside()
    cond_v, _, inverse_v, ratio_v = constants(cond_t, leak_t)
    rate_v = [bind_t[0, i] * DT for i in range(3)]
    tis_at = parts * HALO * width
    conc_at = tis_at + HALO * rows
    ends = edges((rows, lanes))

    def labels_of(side, j):
        return side[tis_at + j * rows : tis_at + (j + 1) * rows, :]

    def halo(side, j, e, valid):
        labels = labels_of(side, j)
        c = select(labels, cond_v) * valid
        level(e, c, ends, kx, ky)
        put(inverse, e, select(labels, inverse_v))
        return c

    low = [halo(from_low, j, j, has_low) for j in range(HALO)] + [select(at(tissue, 0, rows), cond_v)]
    high = [select(at(tissue, layers - 1, rows), cond_v)] + [halo(from_high, j, layers + HALO + j, has_high) for j in range(HALO)]
    for j in range(HALO):
        put(kz, j, low[j] * low[j + 1])
        put(kz, layers + HALO - 1 + j, high[j] * high[j + 1])
    for side, j, layer in ((from_low, HALO - 1, 0), (from_high, 0, layers + 1)):
        put(keep, layer, remaining(select(labels_of(side, j), rate_v), diffuse_t[0] * DT, ends))
    for j in range(TSTEPS):
        span = slice(conc_at + j * rows, conc_at + (j + 1) * rows)
        put(wide, j, from_low[span, :])
        put(wide, layers + TSTEPS + j, from_high[span, :])

    for k in range(parts):
        column = pl.multiple_of((me ^ k) * width, width)

        def spot(layer):
            return pl.ds(pl.multiple_of(layer * rows + column, width), width)

        for i in range(rim):
            top = i + (layers - rim)
            p0[spot(i + HALO), :] = blocks[k * 2 * rim + i] * ratio[spot(i), :]
            p0[spot(top + HALO), :] = blocks[k * 2 * rim + rim + i] * ratio[spot(top), :]
        for j in range(HALO):
            span = slice((k * HALO + j) * width, (k * HALO + j + 1) * width)
            for side, e in ((from_low, j), (from_high, layers + HALO + j)):
                labels = side[pl.ds(pl.multiple_of(tis_at + j * rows + column, width), width), :]
                p0[spot(e), :] = side[span, :] * select(labels, ratio_v)

    faces = (kx, ky, kz)

    for e in range(1, rim + HALO - 1):
        image(e, rows, faces, inverse, p0, u0, p_next)
        image(layers + 2 * HALO - 1 - e, rows, faces, inverse, p0, u0, p_next)
    for e in (HALO - 1, layers + HALO):
        put(u_next, e, following(at(u0, e, rows), 1))

    def sum_over(first, count, totals):
        for i in range(first, first + count):
            totals = products(i + HALO, rows, totals, faces, diag, p0, u0, u_next)
        return totals

    zero = jnp.zeros((8, lanes), jnp.float32)
    totals = sum_over(0, rim - 2, (zero,) * 4)
    totals = sum_over(layers - rim + 1, rim - 1, totals)
    for i in range(4):
        sums[i] = totals[i]


def core_kernel(parts, rim, rows, vp, *refs):
    inner, refs = refs[:parts], refs[parts:]
    kx, ky, kz, diag, inverse, ratio, part = refs[:7]
    p0, u0, p_next, u_next, sums = refs[11:]
    layers, width, _ = vp.shape
    me = lax.axis_index("size")
    sources = [[vp.at[rim : layers - rim]], [inner[0]], [inner[1], inner[2]]] + [[ref] for ref in inner[3:]]
    for k, pieces in enumerate(sources):
        column = pl.multiple_of((me ^ k) * width, width)

        def spot(layer):
            return pl.ds(pl.multiple_of(layer * rows + column, width), width)

        layer = rim
        for piece in pieces:
            for i in range(piece.shape[0]):
                p0[spot(layer + HALO), :] = piece[i] * ratio[spot(layer), :]
                layer += 1

    faces = (kx, ky, kz)
    first = rim + HALO - 1
    last = layers - rim + HALO

    def terms(e, totals):
        return products(e, rows, totals, faces, diag, p0, u0, u_next)

    def picture(e):
        image(e, rows, faces, inverse, p0, u0, p_next)

    def body(i, totals):
        e = first + 2 * i
        totals = terms(e - 2, terms(e - 3, totals))
        picture(e)
        picture(e + 1)
        return totals

    picture(first)
    picture(first + 1)
    pairs = (last + 1 - first) // 2
    totals = lax.fori_loop(1, pairs, body, tuple(part[i] for i in range(4)))
    done = first + 2 * pairs
    for e in range(done, last + 1):
        picture(e)
    for e in range(done - 3, last + 1):
        totals = terms(e, totals)
    sums[...] = jnp.concatenate([t.sum(0, keepdims=True) for t in totals] * 2, 0)


def slide_kernel(rows, wide, low, high):
    def body(i, carry):
        conc = at(wide, i + 1, rows)
        put(low, i, preceding(conc, 1))
        put(high, i, following(conc, 1))
        return carry

    lax.fori_loop(0, low.shape[0] // rows, body, 0, unroll=math.gcd(low.shape[0] // rows, 17))


def transport_kernel(width, rows, hinder_t, diffuse_t, mine, theirs, p0, u0, p_next, u_next, kx, ky, kz, rate, keep, wide, wide_low, wide_high, bound, pressure_hbm, free_hbm, bound_hbm, press, first, kept, zo, zb, xo, xb, yo, yb, pressure, free_out, bound_out, sems):
    lanes = bound.shape[1]
    layers = bound.shape[0] // rows
    me = lax.axis_index("size")
    has_low, has_high = inside()
    sums = mine[...] + theirs[...]
    rho, drop, second, shared = [jnp.sum(sums[i : i + 1, :], axis=1, keepdims=True) for i in range(4)]
    third = second - 2.0 * shared
    alpha = rho / drop
    rho_next = alpha * alpha * second - rho
    beta = rho_next / rho
    curve = drop - 2.0 * alpha * second + alpha * alpha * third - beta * rho_next / alpha
    alpha_next = rho_next / curve
    on_p = jnp.broadcast_to(alpha + alpha_next * (1.0 + beta), (8, lanes))[None]
    on_u = jnp.broadcast_to(-alpha_next * alpha, (8, lanes))[None]
    diffuse = diffuse_t[0] * DT
    hinder = hinder_t[0] * DT

    def combine(p, u, by_p, by_u):
        return (by_p * p.reshape(-1, 8, lanes) + by_u * u.reshape(-1, 8, lanes)).reshape(p.shape)

    def own(i, carry):
        spot = pl.ds(pl.multiple_of((i + HALO) * rows + me * width, width), width)
        put(pressure, i, combine(p0[spot, :], u0[spot, :], on_p, on_u))
        return carry

    lax.fori_loop(0, layers, own, 0, unroll=8)
    drive_p, drive_u = hinder * on_p, hinder * on_u

    def halves(flow, through):
        out = jnp.maximum(flow, 0.0) + through
        return out, out - flow

    def near(ref, layer, shift=0):
        return at(ref, layer, rows, shift)

    def store(ref, layer, value):
        put(ref, layer, value)

    def drive(e):
        store(press, e, combine(near(p0, e), near(u0, e), drive_p, drive_u))

    lane = lax.broadcasted_iota(jnp.int32, (rows, lanes), 1)
    row = lax.broadcasted_iota(jnp.int32, (rows, lanes), 0)
    along = jnp.where(row == rows - 1, 0.0, diffuse)
    rising = jnp.where(lane == lanes - 1, 0.0, diffuse)
    falling = jnp.where(lane == 0, 0.0, diffuse)

    def advance(i, z_out, z_back):
        e = i + TSTEPS
        here, conc = near(press, e), near(wide, i + 1)
        z_up, z_down = halves(near(kz, e) * (here - near(press, e + 1)), diffuse)
        stay = near(keep, i) - z_up - z_back
        moved = z_out * near(wide, i) + z_down * near(wide, i + 2)
        out, back = halves(near(kx, e) * (here - near(press, e, 1)), along)
        into = preceding(out, 0)
        stay = stay - out - preceding(back, 0)
        moved = moved + into * near(wide, i + 1, -1) + back * near(wide, i + 1, 1)
        flow = near(ky, e) * (here - combine(near(p_next, e), near(u_next, e), drive_p, drive_u))
        out, y_back = halves(flow, rising)
        y_into, y_low = halves(preceding(flow, 1), falling)
        stay = stay - out - y_low
        moved = moved + y_into * near(wide_low, i) + y_back * near(wide_high, i)
        for ref, value in ((zo, z_up), (zb, z_down), (xo, into), (xb, back), (yo, y_into), (yb, y_back), (kept, stay)):
            store(ref, i + 1, value)
        valid = jnp.where(i == 0, has_low, jnp.where(i == layers + 1, has_high, 1.0))
        store(first, i + 1, (stay * conc + moved) * valid)
        return z_up, z_down

    def finish(i):
        here = near(first, i + 1)
        result = near(kept, i + 1) * here + near(zo, i) * near(first, i) + near(zb, i + 1) * near(first, i + 2)
        result = result + near(xo, i + 1) * near(first, i + 1, -1) + near(xb, i + 1) * near(first, i + 1, 1)
        result = result + near(yo, i + 1) * preceding(here, 1) + near(yb, i + 1) * following(here, 1)
        store(free_out, i - 1, result)
        gain = near(rate, i - 1) * (near(wide, i + 1) + here)
        store(bound_out, i - 1, near(bound, i - 1) + gain)

    for e in range(TSTEPS - 1, TSTEPS + 3):
        drive(e)
    z_out, z_back = halves(near(kz, TSTEPS - 1) * (near(press, TSTEPS - 1) - near(press, TSTEPS)), diffuse)
    store(zo, 0, z_out)
    store(zb, 0, z_back)

    def two(i):
        z_out, z_back = advance(i, near(zo, i), near(zb, i))
        advance(i + 1, z_out, z_back)
        for step in range(TSTEPS + 3, TSTEPS + 5):
            drive(jnp.minimum(i + step, layers + 2 * TSTEPS))

    def begin(j, carry):
        two(2 * j)
        return carry

    lax.fori_loop(0, 2, begin, 0)

    def body(j, carry):
        finish(2 * j - 3)
        finish(2 * j - 2)
        two(2 * j)
        return carry

    pairs = (layers + 2) // 2
    chunk = layers // 4
    copies = [pltpu.make_async_copy(pressure, pressure_hbm, sems.at[0])]
    copies[0].start()

    def send(first, count):
        span = pl.ds(first * rows, count * rows)
        for here, there in ((free_out, free_hbm), (bound_out, bound_hbm)):
            copy = pltpu.make_async_copy(here.at[span, :], there.at[span, :], sems.at[len(copies)])
            copy.start()
            copies.append(copy)

    done, sent = 2, 0
    for c in range(1, 4):
        until = (c * chunk + 2) // 2 + 1
        lax.fori_loop(done, until, body, 0)
        ready = 2 * until - 4
        send(sent, ready - sent)
        done, sent = until, ready
    lax.fori_loop(done, pairs, body, 0)
    for i in range(2 * pairs, layers + 2):
        advance(i, near(zo, i), near(zb, i))
    for i in range(2 * pairs - 3, layers + 1):
        finish(i)
    send(sent, layers - sent)
    for copy in copies:
        copy.wait()


def swapped(array, axis, bit):
    count = lax.axis_size(axis)
    return lax.ppermute(array, axis, [(i, i ^ bit) for i in range(count)])


def butterfly(array, axis):
    bit = 1
    while bit < lax.axis_size(axis):
        array = jnp.concatenate([array, swapped(array, axis, bit)], 0)
        bit *= 2
    return array


def is_odd():
    return lax.rem(lax.axis_index("gz"), 2) == 1


def across(low, high):
    count = lax.axis_size("gz")
    pairs = [(i, i ^ 1) for i in range(count)]
    near = lax.ppermute(jnp.where(is_odd(), low, high), "gz", pairs)
    pairs = [(i, i + 1) for i in range(1, count - 1, 2)]
    far = lax.ppermute(jnp.where(is_odd(), high, low), "gz", pairs + [(j, i) for i, j in pairs])
    return near, far


def total_over(array, axis):
    count = lax.axis_size(axis)
    step = 1
    while True:
        other = swapped(array, axis, step)
        step *= 2
        if step == count:
            return array, other
        array = array + other


def smem():
    return pl.BlockSpec(memory_space=pltpu.SMEM)


def vmem():
    return pl.BlockSpec(memory_space=pltpu.VMEM)


def f32(*shape):
    return jax.ShapeDtypeStruct(shape, jnp.float32)


def call(kernel, outs, scalars, arrays, scratch=(), aliases={}):
    size = sum(4 * math.prod(a.shape) for a in list(outs) + list(arrays) + list(scratch))
    return pl.pallas_call(
        kernel,
        out_shape=tuple(outs),
        in_specs=[smem()] * len(scalars) + [vmem()] * len(arrays),
        out_specs=(vmem(),) * len(outs),
        scratch_shapes=[pltpu.VMEM(s.shape, s.dtype) for s in scratch],
        input_output_aliases=aliases,
        compiler_params=pltpu.CompilerParams(vmem_limit_bytes=size + (4 << 20)),
    )(*scalars, *arrays)


def program(tissue, vessel_pressure, cond_table, leak_table, bind_table, hindrance, diffusivity, free_conc, bound_conc):
    layers, width, lanes = vessel_pressure.shape
    rows = tissue.shape[1]
    parts = rows // width
    rim = HALO
    conc, bound = free_conc[0], bound_conc[0]
    slab = f32(layers * rows, lanes)
    extended = f32((layers + 2 * HALO) * rows, lanes)
    stepped = f32((layers + 2) * rows, lanes)
    wider = f32((layers + 2 * TSTEPS) * rows, lanes)
    count = layers - 2 * rim
    early = EARLY * count // 32
    rims, middle, ahead, rest = call(
        functools.partial(split_kernel, rim, early),
        [f32(2 * rim, width, lanes), f32(count, width, lanes), f32(early, width, lanes), f32(count - early, width, lanes)],
        [],
        [vessel_pressure],
    )
    blocks = butterfly(rims, "size")
    inner = [(swapped(middle, "size", k),) for k in range(1, parts)]
    inner[1] = (swapped(ahead, "size", 2), swapped(rest, "size", 2))
    inner = [piece for pieces in inner for piece in pieces]
    border = f32((HALO + TSTEPS) * rows, lanes)
    border_low, border_high = pl.pallas_call(
        border_kernel,
        out_shape=(border,) * 2,
        in_specs=[pl.BlockSpec(memory_space=pltpu.HBM)] * 2,
        out_specs=(vmem(),) * 2,
        scratch_shapes=[pltpu.VMEM((2, HALO, rows, lanes), jnp.int32), pltpu.SemaphoreType.DMA((2, 1 + TSTEPS))],
        compiler_params=pltpu.CompilerParams(vmem_limit_bytes=8 << 20),
        name="border",
    )(pltpu.with_memory_space_constraint(tissue, pltpu.HBM), pltpu.with_memory_space_constraint(conc, pltpu.HBM))

    def payload(first, border):
        pieces = [blocks[k * 2 * rim + first : k * 2 * rim + first + HALO] for k in range(parts)] + [border]
        return jnp.concatenate([a.reshape(-1, lanes) for a in pieces], 0)

    near, far = across(payload(0, border_low), payload(2 * rim - HALO, border_high))
    tissue, conc, bound = (a.reshape(-1, lanes) for a in (tissue, conc, bound))
    kx, ky, kz, diag, inverse, ratio, rate, keep, wide = call(
        functools.partial(prepare_kernel, rows),
        [extended] * 3 + [slab, extended, slab, slab, stepped, wider],
        [cond_table, leak_table, bind_table, diffusivity],
        [tissue, conc],
    )
    kx, ky, kz, inverse, keep, wide, p0, u0, p_next, u_next, part = call(
        functools.partial(rim_kernel, parts, rim, width, rows),
        [extended] * 4 + [stepped, wider] + [extended] * 4 + [f32(4, 8, lanes)],
        [cond_table, leak_table, bind_table, diffusivity],
        [blocks, near, far, tissue, diag, ratio, kx, ky, kz, inverse, keep, wide],
        scratch=[f32(*near.shape)] * 2,
        aliases={10 + i: i for i in range(6)},
    )
    p0, u0, p_next, u_next, sums = call(
        functools.partial(core_kernel, parts, rim, rows),
        [extended] * 4 + [f32(8, lanes)],
        [],
        [vessel_pressure, *inner, kx, ky, kz, diag, inverse, ratio, part, p0, u0, p_next, u_next],
        aliases={parts + 8 + i: i for i in range(4)},
    )
    wide_low, wide_high = call(functools.partial(slide_kernel, rows), [stepped] * 2, [], [wide])
    mine, theirs = total_over(sums, "gz")
    operands = [mine, theirs, p0, u0, p_next, u_next, kx, ky, kz, rate, keep, wide, wide_low, wide_high, bound]
    outs = (f32(layers * width, lanes), slab, slab)
    held = [f32((layers + 2 * HALO + 1) * rows, lanes)] + [wider] * 8 + list(outs)
    size = sum(4 * math.prod(a.shape) for a in operands + held)
    pressure, free, bound = pl.pallas_call(
        functools.partial(transport_kernel, width, rows),
        out_shape=outs,
        in_specs=[smem()] * 2 + [vmem()] * len(operands),
        out_specs=(pl.BlockSpec(memory_space=pltpu.HBM),) * 3,
        scratch_shapes=[pltpu.VMEM(a.shape, a.dtype) for a in held] + [pltpu.SemaphoreType.DMA((9,))],
        compiler_params=pltpu.CompilerParams(vmem_limit_bytes=size + (4 << 20)),
        name="transport",
    )(hindrance, diffusivity, *operands)
    shape = (1, layers, rows, lanes)
    return pressure.reshape(layers, width, lanes), free.reshape(shape), bound.reshape(shape)


def solution(mesh):
    return jax.shard_map(
        program,
        mesh=mesh,
        in_specs=(
            P("gz", None, None),
            P("gz", "size", None),
            P(),
            P(),
            P("size", None),
            P("size"),
            P("size"),
            P("size", "gz", None, None),
            P("size", "gz", None, None),
        ),
        out_specs=(P("gz", "size", None), P("size", "gz", None, None), P("size", "gz", None, None)),
        check_vma=False,
    )
```

```python
import functools
import math
import jax
import jax.numpy as jnp
from jax import lax
from jax.experimental import pallas as pl
from jax.experimental.pallas import tpu as pltpu
from jax.sharding import PartitionSpec as P

TSTEPS = 2
HALO = TSTEPS + 1
DT = 0.1
EARLY = 10
GROUP = 4
STRIDE = 4


def select(labels, values):
    return jnp.where(labels == 0, values[0], jnp.where(labels == 1, values[1], values[2]))


def following(cells, axis):
    return pltpu.roll(cells, cells.shape[axis] - 1, axis)


def preceding(cells, axis):
    return pltpu.roll(cells, 1, axis)


def edges(shape):
    row = lax.broadcasted_iota(jnp.int32, shape, 0)
    lane = lax.broadcasted_iota(jnp.int32, shape, 1)
    return (row == 0, row == shape[0] - 1), (lane == 0, lane == shape[1] - 1)


def inside():
    slab = lax.axis_index("gz")
    has_low = (slab > 0).astype(jnp.float32)
    has_high = (slab < lax.axis_size("gz") - 1).astype(jnp.float32)
    return has_low, has_high


def at(ref, layer, rows, shift=0):
    if shift == 0:
        return ref[pl.ds(pl.multiple_of(layer * rows, 8), rows), :]
    view = ref.at[pl.ds(pl.multiple_of(layer * rows - 8, 8), rows + 16), :]
    return view[8 + shift : 8 + shift + rows, :]


def put(ref, layer, value):
    rows = value.shape[0]
    ref[pl.ds(pl.multiple_of(layer * rows, 8), rows), :] = value


def image(e, rows, faces, inverse, p0, u0, p_next):
    kx, ky, kz = faces
    p, y = at(p0, e, rows), at(ky, e, rows)
    ahead = following(p, 1)
    pull = at(kz, e, rows) * at(p0, e + 1, rows) + at(kz, e - 1, rows) * at(p0, e - 1, rows)
    pull = pull + (at(kx, e, rows) * at(p0, e, rows, 1) + at(kx, e, rows, -1) * at(p0, e, rows, -1))
    pull = pull + (y * ahead + preceding(y * p, 1))
    put(p_next, e, ahead)
    put(u0, e, p - at(inverse, e, rows) * pull)


def products(e, rows, totals, faces, diag, p0, u0, u_next):
    kx, ky, kz = faces
    p, u = at(p0, e, rows), at(u0, e, rows)
    d = at(diag, e - HALO, rows)
    dp, du = d * p, d * u
    ahead = following(u, 1)
    pull = at(kz, e, rows) * at(u0, e + 1, rows) + at(kx, e, rows) * at(u0, e, rows, 1) + at(ky, e, rows) * ahead
    put(u_next, e, ahead)
    terms = (dp * p, dp * u, du * u, pull * u)
    return tuple(a + t.reshape(-1, 8, t.shape[-1]).sum(0) for a, t in zip(totals, terms))


def split_kernel(rim, early, vp, rims, inner, ahead, rest):
    layers = vp.shape[0]
    rims[:rim] = vp[:rim]
    rims[rim:] = vp[layers - rim :]
    inner[...] = vp[rim : layers - rim]
    ahead[...] = vp[rim : rim + early]
    rest[...] = vp[rim + early : layers - rim]


def border_kernel(tissue, conc, low, high, labels, sems):
    layers, rows, _ = tissue.shape
    copies = []
    for side, out, first, start in ((0, low, 0, 0), (1, high, layers - HALO, layers - TSTEPS)):
        copies.append(pltpu.make_async_copy(tissue.at[pl.ds(first, HALO)], labels.at[side], sems.at[side, 0]))
        for j in range(TSTEPS):
            spot = pl.ds((HALO + j) * rows, rows)
            copies.append(pltpu.make_async_copy(conc.at[start + j], out.at[spot, :], sems.at[side, 1 + j]))
    for copy in copies:
        copy.start()
    for copy in copies:
        copy.wait()
    for side, out in ((0, low), (1, high)):
        for j in range(HALO):
            out[j * rows : (j + 1) * rows, :] = labels[side, j].astype(jnp.float32)


def constants(cond_t, leak_t):
    cond_v = [cond_t[i] for i in range(3)]
    leak_v = [leak_t[i] for i in range(3)]
    diag_v = [6.0 * c * c + k for c, k in zip(cond_v, leak_v)]
    inverse_v = [1.0 / d for d in diag_v]
    ratio_v = [k / d for k, d in zip(leak_v, diag_v)]
    return cond_v, diag_v, inverse_v, ratio_v


def level(e, c, ends, kx, ky):
    put(kx, e, jnp.where(ends[0][1], 0.0, c * following(c, 0)))
    put(ky, e, jnp.where(ends[1][1], 0.0, c * following(c, 1)))


def remaining(rate, diffuse, ends):
    stay = 1.0 - rate
    for low, high in ends:
        stay = stay - jnp.where(low, diffuse, 0.0) - jnp.where(high, diffuse, 0.0)
    return stay


def prepare_kernel(rows, cond_t, leak_t, bind_t, diffuse_t, tissue, conc, kx, ky, kz, diag, inverse, ratio, rate, keep, wide):
    shape = (rows, tissue.shape[1])
    layers = tissue.shape[0] // rows
    cond_v, diag_v, inverse_v, ratio_v = constants(cond_t, leak_t)
    rate_v = [bind_t[0, i] * DT for i in range(3)]
    ends = edges(shape)
    base = remaining(0.0, diffuse_t[0] * DT, ends)

    def own(i, before):
        e = i + HALO
        labels = at(tissue, i, rows)
        c = select(labels, cond_v)
        r = select(labels, rate_v)
        put(diag, i, select(labels, diag_v))
        put(inverse, e, select(labels, inverse_v))
        put(ratio, i, select(labels, ratio_v))
        put(rate, i, r)
        put(keep, i + 1, base - r)
        put(wide, i + TSTEPS, at(conc, i, rows))
        level(e, c, ends, kx, ky)
        put(kz, e - 1, before * c)
        return c

    lax.fori_loop(0, layers, own, jnp.zeros(shape, jnp.float32), unroll=4)


def rim_kernel(parts, rim, width, rows, cond_t, leak_t, bind_t, diffuse_t, blocks, near, far, tissue, diag, ratio, *refs):
    kx, ky, kz, inverse, keep, wide, p0, u0, p_next, u_next, sums, from_low, from_high = refs[6:]
    odd = is_odd()
    from_low[...] = jnp.where(odd, near[...], far[...])
    from_high[...] = jnp.where(odd, far[...], near[...])
    lanes = tissue.shape[1]
    layers = tissue.shape[0] // rows
    me = lax.axis_index("size")
    has_low, has_high = inside()
    cond_v, _, inverse_v, ratio_v = constants(cond_t, leak_t)
    rate_v = [bind_t[0, i] * DT for i in range(3)]
    tis_at = parts * HALO * width
    conc_at = tis_at + HALO * rows
    ends = edges((rows, lanes))

    def labels_of(side, j):
        return side[tis_at + j * rows : tis_at + (j + 1) * rows, :]

    def halo(side, j, e, valid):
        labels = labels_of(side, j)
        c = select(labels, cond_v) * valid
        level(e, c, ends, kx, ky)
        put(inverse, e, select(labels, inverse_v))
        return c

    low = [halo(from_low, j, j, has_low) for j in range(HALO)] + [select(at(tissue, 0, rows), cond_v)]
    high = [select(at(tissue, layers - 1, rows), cond_v)] + [halo(from_high, j, layers + HALO + j, has_high) for j in range(HALO)]
    for j in range(HALO):
        put(kz, j, low[j] * low[j + 1])
        put(kz, layers + HALO - 1 + j, high[j] * high[j + 1])
    for side, j, layer in ((from_low, HALO - 1, 0), (from_high, 0, layers + 1)):
        put(keep, layer, remaining(select(labels_of(side, j), rate_v), diffuse_t[0] * DT, ends))
    for j in range(TSTEPS):
        span = slice(conc_at + j * rows, conc_at + (j + 1) * rows)
        put(wide, j, from_low[span, :])
        put(wide, layers + TSTEPS + j, from_high[span, :])

    for k in range(parts):
        column = pl.multiple_of((me ^ k) * width, width)

        def spot(layer):
            return pl.ds(pl.multiple_of(layer * rows + column, width), width)

        for i in range(rim):
            top = i + (layers - rim)
            p0[spot(i + HALO), :] = blocks[k * 2 * rim + i] * ratio[spot(i), :]
            p0[spot(top + HALO), :] = blocks[k * 2 * rim + rim + i] * ratio[spot(top), :]
        for j in range(HALO):
            span = slice((k * HALO + j) * width, (k * HALO + j + 1) * width)
            for side, e in ((from_low, j), (from_high, layers + HALO + j)):
                labels = side[pl.ds(pl.multiple_of(tis_at + j * rows + column, width), width), :]
                p0[spot(e), :] = side[span, :] * select(labels, ratio_v)

    faces = (kx, ky, kz)

    for e in range(1, rim + HALO - 1):
        image(e, rows, faces, inverse, p0, u0, p_next)
        image(layers + 2 * HALO - 1 - e, rows, faces, inverse, p0, u0, p_next)
    for e in (HALO - 1, layers + HALO):
        put(u_next, e, following(at(u0, e, rows), 1))

    def sum_over(first, count, totals):
        for i in range(first, first + count):
            totals = products(i + HALO, rows, totals, faces, diag, p0, u0, u_next)
        return totals

    zero = jnp.zeros((8, lanes), jnp.float32)
    totals = sum_over(0, rim - 2, (zero,) * 4)
    totals = sum_over(layers - rim + 1, rim - 1, totals)
    for i in range(4):
        sums[i] = totals[i]


def core_kernel(parts, rim, rows, vp, *refs):
    inner, refs = refs[:parts], refs[parts:]
    kx, ky, kz, diag, inverse, ratio, part = refs[:7]
    p0, u0, p_next, u_next, sums = refs[11:]
    layers, width, _ = vp.shape
    me = lax.axis_index("size")
    sources = [[vp.at[rim : layers - rim]], [inner[0]], [inner[1], inner[2]]] + [[ref] for ref in inner[3:]]
    for k, pieces in enumerate(sources):
        column = pl.multiple_of((me ^ k) * width, width)

        def spot(layer):
            return pl.ds(pl.multiple_of(layer * rows + column, width), width)

        layer = rim
        for piece in pieces:
            for i in range(piece.shape[0]):
                p0[spot(layer + HALO), :] = piece[i] * ratio[spot(layer), :]
                layer += 1

    faces = (kx, ky, kz)
    first = rim + HALO - 1
    last = layers - rim + HALO

    def terms(e, totals):
        return products(e, rows, totals, faces, diag, p0, u0, u_next)

    def picture(e):
        image(e, rows, faces, inverse, p0, u0, p_next)

    def body(i, totals):
        e = first + GROUP * i
        for step in range(GROUP):
            totals = terms(e - GROUP - 1 + step, totals)
        for step in range(GROUP):
            picture(e + step)
        return totals

    for step in range(GROUP):
        picture(first + step)
    groups = (last + 1 - first) // GROUP
    totals = lax.fori_loop(1, groups, body, tuple(part[i] for i in range(4)))
    done = first + GROUP * groups
    for e in range(done, last + 1):
        picture(e)
    for e in range(done - GROUP - 1, last + 1):
        totals = terms(e, totals)
    sums[...] = jnp.concatenate([t.sum(0, keepdims=True) for t in totals] * 2, 0)


def slide_kernel(rows, wide, low, high):
    def body(i, carry):
        conc = at(wide, i + 1, rows)
        put(low, i, preceding(conc, 1))
        put(high, i, following(conc, 1))
        return carry

    lax.fori_loop(0, low.shape[0] // rows, body, 0, unroll=math.gcd(low.shape[0] // rows, 17))


def transport_kernel(width, rows, hinder_t, diffuse_t, mine, theirs, p0, u0, p_next, u_next, kx, ky, kz, rate, keep, wide, wide_low, wide_high, bound, pressure_hbm, free_hbm, bound_hbm, press, first, kept, zo, zb, xo, xb, yo, yb, pressure, free_out, bound_out, sems):
    lanes = bound.shape[1]
    layers = bound.shape[0] // rows
    me = lax.axis_index("size")
    has_low, has_high = inside()
    sums = mine[...] + theirs[...]
    rho, drop, second, shared = [jnp.sum(sums[i : i + 1, :], axis=1, keepdims=True) for i in range(4)]
    third = second - 2.0 * shared
    alpha = rho / drop
    rho_next = alpha * alpha * second - rho
    beta = rho_next / rho
    curve = drop - 2.0 * alpha * second + alpha * alpha * third - beta * rho_next / alpha
    alpha_next = rho_next / curve
    on_p = jnp.broadcast_to(alpha + alpha_next * (1.0 + beta), (8, lanes))[None]
    on_u = jnp.broadcast_to(-alpha_next * alpha, (8, lanes))[None]
    diffuse = diffuse_t[0] * DT
    hinder = hinder_t[0] * DT

    def combine(p, u, by_p, by_u):
        return (by_p * p.reshape(-1, 8, lanes) + by_u * u.reshape(-1, 8, lanes)).reshape(p.shape)

    def own(i, carry):
        spot = pl.ds(pl.multiple_of((i + HALO) * rows + me * width, width), width)
        put(pressure, i, combine(p0[spot, :], u0[spot, :], on_p, on_u))
        return carry

    lax.fori_loop(0, layers, own, 0, unroll=8)
    drive_p, drive_u = hinder * on_p, hinder * on_u

    def halves(flow, through):
        out = jnp.maximum(flow, 0.0) + through
        return out, out - flow

    def near(ref, layer, shift=0):
        return at(ref, layer, rows, shift)

    def store(ref, layer, value):
        put(ref, layer, value)

    def drive(e):
        store(press, e, combine(near(p0, e), near(u0, e), drive_p, drive_u))

    lane = lax.broadcasted_iota(jnp.int32, (rows, lanes), 1)
    row = lax.broadcasted_iota(jnp.int32, (rows, lanes), 0)
    along = jnp.where(row == rows - 1, 0.0, diffuse)
    rising = jnp.where(lane == lanes - 1, 0.0, diffuse)
    falling = jnp.where(lane == 0, 0.0, diffuse)

    def advance(i, z_out, z_back):
        e = i + TSTEPS
        here, conc = near(press, e), near(wide, i + 1)
        z_up, z_down = halves(near(kz, e) * (here - near(press, e + 1)), diffuse)
        stay = near(keep, i) - z_up - z_back
        moved = z_out * near(wide, i) + z_down * near(wide, i + 2)
        out, back = halves(near(kx, e) * (here - near(press, e, 1)), along)
        into = preceding(out, 0)
        stay = stay - out - preceding(back, 0)
        moved = moved + into * near(wide, i + 1, -1) + back * near(wide, i + 1, 1)
        flow = near(ky, e) * (here - combine(near(p_next, e), near(u_next, e), drive_p, drive_u))
        out, y_back = halves(flow, rising)
        y_into, y_low = halves(preceding(flow, 1), falling)
        stay = stay - out - y_low
        moved = moved + y_into * near(wide_low, i) + y_back * near(wide_high, i)
        for ref, value in ((zo, z_up), (zb, z_down), (xo, into), (xb, back), (yo, y_into), (yb, y_back), (kept, stay)):
            store(ref, i + 1, value)
        valid = jnp.where(i == 0, has_low, jnp.where(i == layers + 1, has_high, 1.0))
        store(first, i + 1, (stay * conc + moved) * valid)
        return z_up, z_down

    def finish(i):
        here = near(first, i + 1)
        result = near(kept, i + 1) * here + near(zo, i) * near(first, i) + near(zb, i + 1) * near(first, i + 2)
        result = result + near(xo, i + 1) * near(first, i + 1, -1) + near(xb, i + 1) * near(first, i + 1, 1)
        result = result + near(yo, i + 1) * preceding(here, 1) + near(yb, i + 1) * following(here, 1)
        store(free_out, i - 1, result)
        gain = near(rate, i - 1) * (near(wide, i + 1) + here)
        store(bound_out, i - 1, near(bound, i - 1) + gain)

    for e in range(TSTEPS - 1, TSTEPS + 1 + STRIDE):
        drive(e)
    z_out, z_back = halves(near(kz, TSTEPS - 1) * (near(press, TSTEPS - 1) - near(press, TSTEPS)), diffuse)
    store(zo, 0, z_out)
    store(zb, 0, z_back)

    def several(i):
        z_out, z_back = near(zo, i), near(zb, i)
        for step in range(STRIDE):
            z_out, z_back = advance(i + step, z_out, z_back)
        for step in range(STRIDE):
            drive(jnp.minimum(i + (TSTEPS + 1 + STRIDE + step), layers + 2 * TSTEPS))

    several(0)
    for i in range(1, STRIDE - 1):
        finish(i)
    several(STRIDE)

    def body(j, carry):
        i = STRIDE * j
        for step in range(STRIDE):
            finish(i - STRIDE - 1 + step)
        several(i)
        return carry

    groups = (layers + 2) // STRIDE
    chunk = layers // 4
    copies = [pltpu.make_async_copy(pressure, pressure_hbm, sems.at[0])]
    copies[0].start()

    def send(first, count):
        span = pl.ds(first * rows, count * rows)
        for here, there in ((free_out, free_hbm), (bound_out, bound_hbm)):
            copy = pltpu.make_async_copy(here.at[span, :], there.at[span, :], sems.at[len(copies)])
            copy.start()
            copies.append(copy)

    done, sent = 2, 0
    for c in range(1, 4):
        until = (c * chunk + 1 + STRIDE) // STRIDE + 1
        lax.fori_loop(done, until, body, 0)
        ready = STRIDE * (until - 1) - 2
        send(sent, ready - sent)
        done, sent = until, ready
    lax.fori_loop(done, groups, body, 0)
    for i in range(STRIDE * groups, layers + 2):
        advance(i, near(zo, i), near(zb, i))
    for i in range(STRIDE * groups - STRIDE - 1, layers + 1):
        finish(i)
    send(sent, layers - sent)
    for copy in copies:
        copy.wait()


def swapped(array, axis, bit):
    count = lax.axis_size(axis)
    return lax.ppermute(array, axis, [(i, i ^ bit) for i in range(count)])


def butterfly(array, axis):
    bit = 1
    while bit < lax.axis_size(axis):
        array = jnp.concatenate([array, swapped(array, axis, bit)], 0)
        bit *= 2
    return array


def is_odd():
    return lax.rem(lax.axis_index("gz"), 2) == 1


def across(low, high):
    count = lax.axis_size("gz")
    pairs = [(i, i ^ 1) for i in range(count)]
    near = lax.ppermute(jnp.where(is_odd(), low, high), "gz", pairs)
    pairs = [(i, i + 1) for i in range(1, count - 1, 2)]
    far = lax.ppermute(jnp.where(is_odd(), high, low), "gz", pairs + [(j, i) for i, j in pairs])
    return near, far


def total_over(array, axis):
    count = lax.axis_size(axis)
    step = 1
    while True:
        other = swapped(array, axis, step)
        step *= 2
        if step == count:
            return array, other
        array = array + other


def smem():
    return pl.BlockSpec(memory_space=pltpu.SMEM)


def vmem():
    return pl.BlockSpec(memory_space=pltpu.VMEM)


def f32(*shape):
    return jax.ShapeDtypeStruct(shape, jnp.float32)


def call(kernel, outs, scalars, arrays, scratch=(), aliases={}):
    size = sum(4 * math.prod(a.shape) for a in list(outs) + list(arrays) + list(scratch))
    return pl.pallas_call(
        kernel,
        out_shape=tuple(outs),
        in_specs=[smem()] * len(scalars) + [vmem()] * len(arrays),
        out_specs=(vmem(),) * len(outs),
        scratch_shapes=[pltpu.VMEM(s.shape, s.dtype) for s in scratch],
        input_output_aliases=aliases,
        compiler_params=pltpu.CompilerParams(vmem_limit_bytes=size + (4 << 20)),
    )(*scalars, *arrays)


def program(tissue, vessel_pressure, cond_table, leak_table, bind_table, hindrance, diffusivity, free_conc, bound_conc):
    layers, width, lanes = vessel_pressure.shape
    rows = tissue.shape[1]
    parts = rows // width
    rim = HALO
    conc, bound = free_conc[0], bound_conc[0]
    slab = f32(layers * rows, lanes)
    extended = f32((layers + 2 * HALO) * rows, lanes)
    stepped = f32((layers + 2) * rows, lanes)
    wider = f32((layers + 2 * TSTEPS) * rows, lanes)
    count = layers - 2 * rim
    early = EARLY * count // 32
    rims, middle, ahead, rest = call(
        functools.partial(split_kernel, rim, early),
        [f32(2 * rim, width, lanes), f32(count, width, lanes), f32(early, width, lanes), f32(count - early, width, lanes)],
        [],
        [vessel_pressure],
    )
    blocks = butterfly(rims, "size")
    inner = [(swapped(middle, "size", k),) for k in range(1, parts)]
    inner[1] = (swapped(ahead, "size", 2), swapped(rest, "size", 2))
    inner = [piece for pieces in inner for piece in pieces]
    border = f32((HALO + TSTEPS) * rows, lanes)
    border_low, border_high = pl.pallas_call(
        border_kernel,
        out_shape=(border,) * 2,
        in_specs=[pl.BlockSpec(memory_space=pltpu.HBM)] * 2,
        out_specs=(vmem(),) * 2,
        scratch_shapes=[pltpu.VMEM((2, HALO, rows, lanes), jnp.int32), pltpu.SemaphoreType.DMA((2, 1 + TSTEPS))],
        compiler_params=pltpu.CompilerParams(vmem_limit_bytes=8 << 20),
        name="border",
    )(pltpu.with_memory_space_constraint(tissue, pltpu.HBM), pltpu.with_memory_space_constraint(conc, pltpu.HBM))

    def payload(first, border):
        pieces = [blocks[k * 2 * rim + first : k * 2 * rim + first + HALO] for k in range(parts)] + [border]
        return jnp.concatenate([a.reshape(-1, lanes) for a in pieces], 0)

    near, far = across(payload(0, border_low), payload(2 * rim - HALO, border_high))
    tissue, conc, bound = (a.reshape(-1, lanes) for a in (tissue, conc, bound))
    kx, ky, kz, diag, inverse, ratio, rate, keep, wide = call(
        functools.partial(prepare_kernel, rows),
        [extended] * 3 + [slab, extended, slab, slab, stepped, wider],
        [cond_table, leak_table, bind_table, diffusivity],
        [tissue, conc],
    )
    kx, ky, kz, inverse, keep, wide, p0, u0, p_next, u_next, part = call(
        functools.partial(rim_kernel, parts, rim, width, rows),
        [extended] * 4 + [stepped, wider] + [extended] * 4 + [f32(4, 8, lanes)],
        [cond_table, leak_table, bind_table, diffusivity],
        [blocks, near, far, tissue, diag, ratio, kx, ky, kz, inverse, keep, wide],
        scratch=[f32(*near.shape)] * 2,
        aliases={10 + i: i for i in range(6)},
    )
    p0, u0, p_next, u_next, sums = call(
        functools.partial(core_kernel, parts, rim, rows),
        [extended] * 4 + [f32(8, lanes)],
        [],
        [vessel_pressure, *inner, kx, ky, kz, diag, inverse, ratio, part, p0, u0, p_next, u_next],
        aliases={parts + 8 + i: i for i in range(4)},
    )
    wide_low, wide_high = call(functools.partial(slide_kernel, rows), [stepped] * 2, [], [wide])
    mine, theirs = total_over(sums, "gz")
    operands = [mine, theirs, p0, u0, p_next, u_next, kx, ky, kz, rate, keep, wide, wide_low, wide_high, bound]
    outs = (f32(layers * width, lanes), slab, slab)
    held = [f32((layers + 2 * HALO + 1) * rows, lanes)] + [wider] * 8 + list(outs)
    size = sum(4 * math.prod(a.shape) for a in operands + held)
    pressure, free, bound = pl.pallas_call(
        functools.partial(transport_kernel, width, rows),
        out_shape=outs,
        in_specs=[smem()] * 2 + [vmem()] * len(operands),
        out_specs=(pl.BlockSpec(memory_space=pltpu.HBM),) * 3,
        scratch_shapes=[pltpu.VMEM(a.shape, a.dtype) for a in held] + [pltpu.SemaphoreType.DMA((9,))],
        compiler_params=pltpu.CompilerParams(vmem_limit_bytes=size + (4 << 20)),
        name="transport",
    )(hindrance, diffusivity, *operands)
    shape = (1, layers, rows, lanes)
    return pressure.reshape(layers, width, lanes), free.reshape(shape), bound.reshape(shape)


def solution(mesh):
    return jax.shard_map(
        program,
        mesh=mesh,
        in_specs=(
            P("gz", None, None),
            P("gz", "size", None),
            P(),
            P(),
            P("size", None),
            P("size"),
            P("size"),
            P("size", "gz", None, None),
            P("size", "gz", None, None),
        ),
        out_specs=(P("gz", "size", None), P("size", "gz", None, None), P("size", "gz", None, None)),
        check_vma=False,
    )
```
